256 devices in a mesh: ctx: 16 (over y, x), tp: 16 (over z, core).
Axes of the slice: x: 4, y: 4, z: 8, core: 2. Of those that a mesh axis runs over, the one named last changes fastest.
Arguments:
- x_input: bfloat16 [4096, 8192], P('ctx', 'tp'), may hold values from -6 to 6
- z_input: bfloat16 [4096, 8192], P('ctx', 'tp'), may hold values from -6 to 6
- bc_input: bfloat16 [4096, 2048], P('ctx', 'tp'), may hold values from -6 to 6
- dt_input: float32 [4096, 128], P('ctx', 'tp'), may hold values from -6 to 6
- decay_log: float32 [128], P('tp'), may hold values from -12 to -2
- skip_weight: float32 [128], P('tp'), may hold values from 0.5 to 2
- conv_x: float32 [4, 8192], P(None, 'tp'), may hold values from -3 to 3
- conv_bc: float32 [4, 2048], replicated, may hold values from -3 to 3
- conv_bias_x: float32 [8192], P('tp'), may hold values from -3 to 3
- conv_bias_bc: float32 [2048], replicated, may hold values from -3 to 3
- norm_gain: float32 [8192], P('tp'), may hold values from 0.1 to 1.9
- out_weight: bfloat16 [8192, 8192], P('tp'), may hold values from -0.0625 to 0.0625
Outputs:
- mixed: bfloat16 [4096, 8192], P('ctx', 'tp')
The draws below stay inside these ranges and needn't reach their ends.
All inputs are finite; a program needn't handle non-finite values.
Results may differ from the reference program's by a relative error of at most 0.0055.
Values may be sent and summed in bfloat16 or wider, within the bound.
No kernel may reach another device: no remote copies, remote signals or barrier semaphores. Data moves between devices by JAX's collectives and lax.ppermute only.
A program may use at most 128 MiB of HBM per device.

```python
import math
import jax
import jax.numpy as jnp
from jax import lax

D = 8192
HEAD = 64
STATE = 128
KERNEL = 4
TOK_DEV = 256
HEADS = 128
GROUPS = 8
INNER = 8192
SEQ = 4096


def draw_decay_log(key, part):
    first_key, second_key, third_key = jax.random.split(jax.random.fold_in(key, 17), 3)
    share = 0.5
    slow_low, slow_high = (0.3, 1.5)
    quick_heads = jax.random.uniform(first_key, (HEADS,), jnp.float32) < share
    quick = jax.random.uniform(second_key, (HEADS,), jnp.float32, math.log(0.03), math.log(0.06))
    slow = jnp.log(jax.random.uniform(third_key, (HEADS,), jnp.float32, slow_low, slow_high) / SEQ)
    return jnp.where(quick_heads, quick, slow).astype(jnp.float32)


def draw_dt_input(key, part):
    level_key, head_key, noise_key = jax.random.split(jax.random.fold_in(key, 29), 3)
    block_count = SEQ // TOK_DEV
    level = jax.random.uniform(level_key, (block_count, 1), jnp.float32, -2.5, 2.5)
    head_level = jax.random.uniform(head_key, (block_count, HEADS), jnp.float32, -0.5, 0.5)
    offsets = jnp.repeat(level + head_level, TOK_DEV, axis=0)
    noise = jax.random.normal(noise_key, (SEQ, HEADS), jnp.float32)
    return jnp.clip(offsets + noise, -6.0, 6.0).astype(jnp.float32)


def shard_levels(rng, extent, cuts, low, top_value):
    gain, own = 1.0, jax.random.fold_in(rng, 6)
    for axis_at, parts in cuts:
        draws = jnp.exp(jax.random.uniform(jax.random.fold_in(own, axis_at), (parts,), jnp.float32, low / len(cuts), top_value / len(cuts)))
        gain = gain * jnp.repeat(draws, extent[axis_at] // parts).reshape([-1 if axis == axis_at else 1 for axis in range(len(extent))])
    return gain


def centred(own_key, extent, scale, most, cuts=(), kind=jnp.bfloat16):
    level = shard_levels(own_key, extent, cuts, -0.22, 0.18) if cuts else 1.0
    values = jax.random.normal(own_key, extent, jnp.float32) * scale * level
    return jnp.minimum(jnp.maximum(values, -most), most).astype(kind)


def setup_inputs(seed: int = 0) -> dict:
    key_of = jax.random.split(jax.random.key(seed), 13)
    return {
        "x_input": centred(key_of[0], (SEQ, INNER), 1.0, 6.0, ((0, 16), (1, 16))),
        "z_input": centred(key_of[1], (SEQ, INNER), 1.0, 6.0, ((0, 16), (1, 16))),
        "bc_input": centred(key_of[2], (SEQ, 2 * GROUPS * STATE), 1.0, 6.0, ((0, 16), (1, 16))),
        "dt_input": draw_dt_input(jax.random.fold_in(key_of[12], 71), 0),
        "decay_log": draw_decay_log(jax.random.fold_in(key_of[12], 71), 0),
        "skip_weight": jnp.clip(jnp.exp(math.log(2.0) - 1.3862944 * jax.random.uniform(key_of[5], (HEADS,), jnp.float32) ** shard_levels(key_of[5], (HEADS,), ((0, 16),), -0.2, 0.2)), 0.5, 2.0),
        "conv_x": centred(key_of[6], (KERNEL, INNER), KERNEL ** -0.5, 3.0, ((1, 16),), jnp.float32),
        "conv_bc": centred(key_of[7], (KERNEL, 2 * GROUPS * STATE), KERNEL ** -0.5, 3.0, (), jnp.float32),
        "conv_bias_x": centred(key_of[8], (INNER,), 0.5, 3.0, ((0, 16),), jnp.float32),
        "conv_bias_bc": centred(key_of[9], (2 * GROUPS * STATE,), 0.5, 3.0, (), jnp.float32),
        "norm_gain": jnp.clip(1.0 + 0.18 * jax.random.normal(key_of[10], (INNER,), jnp.float32), 0.1, 1.9),
        "out_weight": centred(key_of[11], (INNER, D), INNER ** -0.5, 0.0625, ((0, 16),)),
    }


HIGH = lax.Precision.HIGHEST

def causal_conv(raw, kernel, offset):
    values = raw.astype(jnp.float32)
    reach = kernel.shape[0] - 1
    padded = jnp.concatenate([jnp.zeros((reach, values.shape[1]), jnp.float32), values], axis=0)
    length = values.shape[0]
    total = offset[None, :] + kernel[0][None, :] * padded[0:length]
    for step in range(1, kernel.shape[0]):
        total = total + kernel[step][None, :] * padded[step:step + length]
    return jax.nn.silu(total)

def reference(x_input, z_input, bc_input, dt_input, decay_log, skip_weight, conv_x, conv_bc, conv_bias_x, conv_bias_bc, norm_gain, out_weight):
    xs = causal_conv(x_input, conv_x, conv_bias_x)
    bcs = causal_conv(bc_input, conv_bc, conv_bias_bc).reshape(SEQ, GROUPS, 2, STATE)
    b_all = bcs[:, :, 0, :]
    c_all = bcs[:, :, 1, :]
    step_size = jax.nn.softplus(dt_input)
    decay_rate = -jnp.exp(decay_log)
    per_group = HEADS // GROUPS
    heads_x = xs.reshape(SEQ, HEADS, HEAD)
    blocks = SEQ // TOK_DEV
    lower = jnp.tril(jnp.ones((TOK_DEV, TOK_DEV), dtype=bool))

    def split_blocks(array):
        return array.reshape((blocks, TOK_DEV) + array.shape[1:])

    def block_step(state, pieces):
        block_x, block_b, block_c, block_dt = pieces
        running = jnp.cumsum(block_dt * decay_rate[None, :], axis=0)
        intersection = jnp.einsum('tgn,sgn->gts', block_c, block_b, precision=HIGH)
        intersection = jnp.repeat(intersection, per_group, axis=0)
        gap = running.T[:, :, None] - running.T[:, None, :]
        weights = jnp.where(lower[None], jnp.exp(jnp.minimum(gap, 0.0)), 0.0) * intersection * block_dt.T[:, None, :]
        local_out = jnp.einsum('hts,shp->thp', weights, block_x, precision=HIGH)
        head_b = jnp.repeat(block_b, per_group, axis=1)
        head_c = jnp.repeat(block_c, per_group, axis=1)
        carried = jnp.einsum('thn,hpn->thp', head_c, state, precision=HIGH) * jnp.exp(running)[:, :, None]
        output = local_out + carried + skip_weight[None, :, None] * block_x
        closing = jnp.exp(running[-1][None, :] - running) * block_dt
        local_state = jnp.einsum('sh,shp,shn->hpn', closing, block_x, head_b, precision=HIGH)
        new_state = jnp.exp(running[-1])[:, None, None] * state + local_state
        return (new_state, output)
    start_state = jnp.zeros((HEADS, HEAD, STATE), jnp.float32)
    ignored, outputs = lax.scan(block_step, start_state, (split_blocks(heads_x), split_blocks(b_all), split_blocks(c_all), split_blocks(step_size)))
    ssm_out = outputs.reshape(SEQ, INNER)
    gated = ssm_out * jax.nn.silu(z_input.astype(jnp.float32))
    meansq = lax.optimization_barrier(jnp.mean(gated * gated, axis=1))
    hidden = (gated * norm_gain[None, :]).astype(jnp.bfloat16)
    projected = jnp.dot(hidden, out_weight, preferred_element_type=jnp.float32)
    return (projected * lax.rsqrt(meansq + 1e-05)[:, None]).astype(jnp.bfloat16)
```

```python
import jax
import jax.numpy as jnp
from jax import lax
from jax.experimental import pallas as pl
from jax.experimental.pallas import tpu as pltpu
from jax.sharding import PartitionSpec as P


bf16 = jnp.bfloat16
f32 = jnp.float32
HIGH = lax.Precision.HIGHEST
AXES = ("ctx", "tp")
NX, NY, NZ = 4, 4, 8
TOK = 256
CH = 512
HD = 8
ST = 128
TILE = 128


def permute(value, target):
    pairs = []
    for ctx in range(NX * NY):
        for z in range(NZ):
            for c in range(2):
                to = target(ctx, z, c)
                if to is not None:
                    pairs.append((ctx * 16 + z * 2 + c, to[0] * 16 + (to[1] % NZ) * 2 + to[2]))
    return lax.ppermute(value, AXES, pairs)


def next_block(value):
    return permute(value, lambda k, z, c: (k + 1, z, c) if k < 15 else None)


def next_block_other(value):
    return permute(value, lambda k, z, c: (k + 1, z, 1 - c) if k < 15 else None)


def other_core(value):
    return permute(value, lambda k, z, c: (k, z, 1 - c))


def up(value):
    return permute(value, lambda k, z, c: (k, z + 1, c))


def down(value):
    return permute(value, lambda k, z, c: (k, z - 1, c))


def flip(value, mask):
    return permute(value, lambda k, z, c: (k, z ^ mask, c))


def silu(v):
    return v / (1.0 + jnp.exp(-v))


def dot(a, b, dims, precision=None):
    return lax.dot_general(a, b, (dims, ((), ())), precision=precision, preferred_element_type=f32)


def parts(v):
    high = v.astype(bf16)
    return high, (v - high.astype(f32)).astype(bf16)


def dot3(a, b, dims):
    ah, al = parts(a)
    bh, bl = parts(b)
    return dot(ah, bh, dims) + (dot(ah, bl, dims) + dot(al, bh, dims))


def spread(cols, first):
    lane = lax.broadcasted_iota(jnp.int32, (cols.shape[0], TILE), 1)
    return jnp.where(lane < 64, cols[:, first : first + 1], cols[:, first + 1 : first + 2])


def conv(ref, tile, taps, bias):
    total = bias
    for k in range(4):
        total = total + taps[k : k + 1] * ref[13 + k : 13 + k + TOK, tile]
    return silu(total)


def local_kernel(
    pos, x, bc, bo, tails, tail_o, dt, dt_t, dl, dl_t, wx, bx, wbc, bbc,
    pay, xs_out, b_out, c_out, cum_out, cum_t_out, dts_out, dts_t_out, joined, joined_bc,
):
    even = pos[1] == 0
    joined[0:16] = tails[:, 0:CH].astype(f32)
    joined[16:] = x[...].astype(f32)
    own, oth = bc[...].astype(f32), bo[...].astype(f32)
    own_t, oth_t = tails[:, CH:].astype(f32), tail_o[...].astype(f32)
    joined_bc[16:, 0:ST] = jnp.where(even, own, oth)
    joined_bc[16:, ST:] = jnp.where(even, oth, own)
    joined_bc[0:16, 0:ST] = jnp.where(even, own_t, oth_t)
    joined_bc[0:16, ST:] = jnp.where(even, oth_t, own_t)
    b = conv(joined_bc, slice(0, ST), wbc[:, 0:ST], bbc[:, 0:ST])
    c = conv(joined_bc, slice(ST, 2 * ST), wbc[:, ST:], bbc[:, ST:])
    b_out[...] = b
    c_out[...] = c
    dts = jnp.logaddexp(dt[...], 0.0)
    dts_t = jnp.logaddexp(dt_t[...], 0.0)
    dts_out[...] = dts
    dts_t_out[...] = dts_t
    row = lax.broadcasted_iota(jnp.int32, (TOK, TOK), 0)
    col = lax.broadcasted_iota(jnp.int32, (TOK, TOK), 1)
    tri = (row >= col).astype(f32)
    tri_t = (row <= col).astype(f32)
    cum = dot(tri, dts * -jnp.exp(dl[...]), ((1,), (0,)), HIGH)
    cum_out[...] = cum
    cum_t_out[...] = dot(dts_t * -jnp.exp(dl_t[...]), tri_t, ((1,), (0,)), HIGH)
    last = cum[TOK - 1 : TOK]
    closing = jnp.exp(last - cum) * dts
    carry = jnp.exp(last)
    bh, bl = parts(b)
    for j in range(4):
        tile = slice(j * TILE, (j + 1) * TILE)
        xs = conv(joined, tile, wx[:, tile], bx[:, tile])
        xs_out[:, tile] = xs
        wh, wl = parts(xs * spread(closing, 2 * j))
        over = ((0,), (0,))
        state = dot(wh, bh, over) + (dot(wh, bl, over) + dot(wl, bh, over))
        for i in range(4):
            pay[4 * j + i, 0:32] = state[32 * i : 32 * i + 32].astype(bf16)
            head = 2 * j + i // 2
            value = jnp.broadcast_to(carry[:, head : head + 1], (16, ST))
            high = value.astype(bf16).astype(f32)
            sub = lax.broadcasted_iota(jnp.int32, (16, ST), 0)
            pay[4 * j + i, 32:48] = jnp.where(sub == 0, high, value - high).astype(bf16)


def inner_kernel(xs, b, c, cum, cum_t, dts, z, sk, a_out, e_out, m_ref):
    cb = dot3(c[...], b[...], ((1,), (1,)))
    cum_c = cum[...]
    cum_r = cum_t[...]
    grow = jnp.exp(cum_c)
    dts_c = dts[...]
    row = lax.broadcasted_iota(jnp.int32, (TILE, TILE), 0)
    col = lax.broadcasted_iota(jnp.int32, (TILE, TILE), 1)
    lower = row >= col
    half = (slice(0, TILE), slice(TILE, TOK))
    lane = lax.broadcasted_iota(jnp.int32, (TILE, TILE), 1)
    for j in range(4):
        tile = slice(j * TILE, (j + 1) * TILE)
        x_tile = xs[:, tile]
        x_dt = (x_tile * spread(dts_c, 2 * j)).astype(bf16)
        gate = silu(z[:, tile].astype(f32))
        grown = spread(grow, 2 * j)
        for i in range(2):
            ys = []
            for h in (2 * j, 2 * j + 1):
                cols = []
                for k in range(i + 1):
                    gap = cum_c[half[i], h : h + 1] - cum_r[h : h + 1, half[k]]
                    if k == i:
                        w = jnp.where(lower, jnp.exp(jnp.minimum(gap, 0.0)), 0.0)
                    else:
                        w = jnp.exp(jnp.minimum(gap, 0.0))
                    cols.append((w * cb[half[i], half[k]]).astype(bf16))
                y = dot(cols[0], x_dt[half[0]], ((1,), (0,)))
                if i == 1:
                    y = y + dot(cols[1], x_dt[half[1]], ((1,), (0,)))
                ys.append(y)
            y = jnp.where(lane < 64, ys[0], ys[1])
            skip = jnp.where(lane[0:1] < 64, sk[:, 2 * j : 2 * j + 1], sk[:, 2 * j + 1 : 2 * j + 2])
            g = gate[half[i]]
            a_out[half[i], tile] = (y + skip * x_tile[half[i]]) * g
            e_out[half[i], tile] = grown[half[i]] * g


def scan_kernel(got, out):
    state = jnp.zeros((32, ST), f32)
    for k in range(16):
        out[k] = state.astype(bf16)
        if k < 15:
            carry = got[k, 32:33].astype(f32) + got[k, 33:34].astype(f32)
            state = carry * state + got[k, 0:32].astype(f32)


def gate_kernel(s, c, a, e, gain, h_out, sq_out):
    ch, cl = parts(c[...])
    ones = jnp.ones((8, TILE), f32)
    total = jnp.zeros((8, TOK), f32)
    for j in range(4):
        tile = slice(j * TILE, (j + 1) * TILE)
        st = s[tile]
        carried = dot(ch, st, ((1,), (1,))) + dot(cl, st, ((1,), (1,)))
        gated = a[:, tile] + e[:, tile] * carried
        h_out[:, tile] = (gated * gain[:, tile]).astype(bf16)
        total = total + dot(ones, gated * gated, ((1,), (1,)), HIGH)
    sq_out[...] = total


def product_kernel(index, own, oth, w_own, w_oth, out):
    total = dot(own[...], w_own[...], ((1,), (0,))) + dot(oth[...], w_oth[...], ((1,), (0,)))
    out[...] = total.astype(out.dtype)


def products(index, own, oth, w_own, w_oth, count, dtype):
    return pl.pallas_call(
        product_kernel,
        grid_spec=pltpu.PrefetchScalarGridSpec(
            num_scalar_prefetch=1,
            grid=(count,),
            in_specs=[
                pl.BlockSpec((TOK, CH), lambda i, at: (0, 0)),
                pl.BlockSpec((TOK, CH), lambda i, at: (0, 0)),
                pl.BlockSpec((CH, CH), lambda i, at: (0, at[i])),
                pl.BlockSpec((CH, CH), lambda i, at: (0, at[i])),
            ],
            out_specs=pl.BlockSpec((None, TOK, CH), lambda i, at: (i, 0, 0)),
        ),
        out_shape=jax.ShapeDtypeStruct((count, TOK, CH), dtype),
    )(index, own, oth, w_own, w_oth)


def whole(shape):
    return jax.ShapeDtypeStruct(shape, f32)


def shards(x, z, bc, dt, decay_log, skip, conv_x, conv_bc, bias_x, bias_bc, gain, w):
    rank = lax.axis_index("tp")
    zi, ci = rank // 2, rank % 2
    pos = jnp.stack([zi, ci]).astype(jnp.int32)

    bo = other_core(bc)
    tails = next_block(jnp.concatenate([x[TOK - 16 :], bc[TOK - 16 :]], axis=1))
    tail_o = next_block_other(bc[TOK - 16 :])
    w_other = other_core(w)

    vmem = pl.BlockSpec(memory_space=pltpu.VMEM)

    def at(shape):
        return pl.BlockSpec(shape, lambda i, p: (0,) * len(shape))

    shapes_in = [
        (TOK, CH), (TOK, ST), (TOK, ST), (16, CH + ST), (16, ST), (TOK, HD), (HD, TOK),
        (1, HD), (HD, 1), (4, CH), (1, CH),
    ]
    local_outs = [
        jax.ShapeDtypeStruct((16, 48, ST), bf16),
        whole((TOK, CH)), whole((TOK, ST)), whole((TOK, ST)),
        whole((TOK, HD)), whole((HD, TOK)), whole((TOK, HD)), whole((HD, TOK)),
    ]
    pay, xs, b, c, cum, cum_t, dts, _ = pl.pallas_call(
        local_kernel,
        grid_spec=pltpu.PrefetchScalarGridSpec(
            num_scalar_prefetch=1,
            grid=(1,),
            in_specs=[at(s) for s in shapes_in]
            + [
                pl.BlockSpec((4, 2 * ST), lambda i, p: (0, p[0])),
                pl.BlockSpec((1, 2 * ST), lambda i, p: (0, p[0])),
            ],
            out_specs=[at(o.shape) for o in local_outs],
            scratch_shapes=[pltpu.VMEM((TOK + 16, CH), f32), pltpu.VMEM((TOK + 16, 2 * ST), f32)],
        ),
        out_shape=local_outs,
    )(
        pos, x, bc, bo, tails, tail_o, dt, dt.T, decay_log[None], decay_log[:, None],
        conv_x, bias_x[None], conv_bc, bias_bc[None],
    )

    got = lax.all_to_all(pay, "ctx", 0, 0, tiled=True)
    a, e = pl.pallas_call(
        inner_kernel,
        out_shape=[whole((TOK, CH)), whole((TOK, CH))],
        in_specs=[vmem] * 8,
        out_specs=[vmem, vmem],
        scratch_shapes=[pltpu.VMEM((8, TILE), f32)],
    )(xs, b, c, cum, cum_t, dts, z, skip[None])
    back = pl.pallas_call(
        scan_kernel,
        out_shape=jax.ShapeDtypeStruct((16, 32, ST), bf16),
        in_specs=[vmem],
        out_specs=vmem,
    )(got)
    incoming = lax.all_to_all(back, "ctx", 0, 0, tiled=True).reshape(CH, ST)
    hidden, squares = pl.pallas_call(
        gate_kernel,
        out_shape=[jax.ShapeDtypeStruct((TOK, CH), bf16), whole((8, TOK))],
        in_specs=[vmem] * 5,
        out_specs=[vmem, vmem],
    )(incoming, c, a, e, gain[None])

    hidden_o = other_core(hidden)
    total = squares + other_core(squares)
    for mask in (1, 2, 4):
        total = total + flip(total, mask)
    scale = lax.rsqrt(total[0] / (NZ * 2 * CH) + 1e-05)

    def column(d):
        return ((zi + d) % NZ) * 2 + ci

    order = (3, 5, 2, 6, 1, 7, 0)
    far = products(jnp.stack([column(4)]).astype(jnp.int32), hidden, hidden_o, w, w_other, 1, bf16)[0]
    near = products(
        jnp.stack([column(d) for d in order]).astype(jnp.int32), hidden, hidden_o, w, w_other, 7, f32
    )
    half = TOK // 2
    f, g = up(far[:half]), down(far[half:])
    f = (near[0] + jnp.pad(f.astype(f32), ((0, half), (0, 0)))).astype(bf16)
    g = (near[1] + jnp.pad(g.astype(f32), ((half, 0), (0, 0)))).astype(bf16)
    f, g = up(f), down(g)
    f, g = (near[2] + f.astype(f32)).astype(bf16), (near[3] + g.astype(f32)).astype(bf16)
    f, g = up(f), down(g)
    f, g = (near[4] + f.astype(f32)).astype(bf16), (near[5] + g.astype(f32)).astype(bf16)
    f, g = up(f), down(g)
    summed = near[6] + f.astype(f32) + g.astype(f32)
    return (summed * scale[:, None]).astype(bf16)


def solution(mesh):
    return jax.shard_map(
        shards,
        mesh=mesh,
        in_specs=(
            P("ctx", "tp"),
            P("ctx", "tp"),
            P("ctx", "tp"),
            P("ctx", "tp"),
            P("tp"),
            P("tp"),
            P(None, "tp"),
            P(),
            P("tp"),
            P(),
            P("tp"),
            P("tp", None),
        ),
        out_specs=P("ctx", "tp"),
        check_vma=False,
    )
```

```python
from functools import partial

import jax
import jax.numpy as jnp
from jax import lax
from jax.experimental import pallas as pl
from jax.experimental.pallas import tpu as pltpu
from jax.sharding import PartitionSpec as P


bf16 = jnp.bfloat16
f32 = jnp.float32
HIGH = lax.Precision.HIGHEST
AXES = ("ctx", "tp")
NX, NY, NZ = 4, 4, 8
TOK = 256
CH = 512
HD = 8
ST = 128
TILE = 128


def permute(value, target):
    pairs = []
    for ctx in range(NX * NY):
        for z in range(NZ):
            for c in range(2):
                to = target(ctx, z, c)
                if to is not None:
                    pairs.append((ctx * 16 + z * 2 + c, to[0] * 16 + (to[1] % NZ) * 2 + to[2]))
    return lax.ppermute(value, AXES, pairs)


def next_block(value):
    return permute(value, lambda k, z, c: (k + 1, z, c) if k < 15 else None)


def other_core(value):
    return permute(value, lambda k, z, c: (k, z, 1 - c))


def up(value):
    return permute(value, lambda k, z, c: (k, z + 1, c))


def down(value):
    return permute(value, lambda k, z, c: (k, z - 1, c))


def silu(v):
    return v / (1.0 + jnp.exp(-v))


def dot(a, b, dims, precision=None):
    return lax.dot_general(a, b, (dims, ((), ())), precision=precision, preferred_element_type=f32)


def parts(v):
    high = v.astype(bf16)
    return high, (v - high.astype(f32)).astype(bf16)


def dot3(a, b, dims):
    ah, al = parts(a)
    bh, bl = parts(b)
    return dot(ah, bh, dims) + (dot(ah, bl, dims) + dot(al, bh, dims))


def spread(cols, first):
    lane = lax.broadcasted_iota(jnp.int32, (cols.shape[0], TILE), 1)
    return jnp.where(lane < 64, cols[:, first : first + 1], cols[:, first + 1 : first + 2])


def conv(ref, tile, taps, bias, first, rows):
    total = bias
    for k in range(4):
        total = total + taps[k : k + 1] * ref[first - 3 + k : first - 3 + k + rows, tile]
    return silu(total)


def taps_of(pos, wbc, bbc):
    group = pl.ds(pl.multiple_of(pos[0] * 2 * ST, 2 * ST), 2 * ST)
    return wbc[:, group], bbc[:, group]


def local_kernel(
    pos, x, bc, bo, dt_t, dl, wx, bx, wbc, bbc,
    xs_out, b_out, c_out, cum_out, dts_out, state_out, xh_out, bch_out, joined, joined_bc,
):
    even = pos[1] == 0
    joined[0:16] = jnp.zeros((16, CH), f32)
    joined[16:] = x[...].astype(f32)
    own, oth = bc[...].astype(f32), bo[...].astype(f32)
    joined_bc[0:16] = jnp.zeros((16, 2 * ST), f32)
    joined_bc[16:, 0:ST] = jnp.where(even, own, oth)
    joined_bc[16:, ST:] = jnp.where(even, oth, own)
    xh_out[...] = joined[16:32]
    bch_out[...] = joined_bc[16:32]
    taps, bias = taps_of(pos, wbc, bbc)
    b = conv(joined_bc, slice(0, ST), taps[:, 0:ST], bias[:, 0:ST], 16, TOK)
    c = conv(joined_bc, slice(ST, 2 * ST), taps[:, ST:], bias[:, ST:], 16, TOK)
    b_out[...] = b
    c_out[...] = c
    dts = jnp.logaddexp(dt_t[...], 0.0).T
    dts_out[...] = dts
    row = lax.broadcasted_iota(jnp.int32, (TOK, TOK), 0)
    col = lax.broadcasted_iota(jnp.int32, (TOK, TOK), 1)
    cum = dot((row >= col).astype(f32), dts * -jnp.exp(dl[...]), ((1,), (0,)), HIGH)
    cum_out[...] = cum
    closing = jnp.exp(cum[TOK - 1 : TOK] - cum) * dts
    late = lax.broadcasted_iota(jnp.int32, (TOK, HD), 0) >= 8
    closing = jnp.where(late, closing, 0.0)
    bh, bl = parts(b)
    over = ((0,), (0,))
    for j in range(4):
        tile = slice(j * TILE, (j + 1) * TILE)
        xs = conv(joined, tile, wx[:, tile], bx[:, tile], 16, TOK)
        xs_out[:, tile] = xs
        wh, wl = parts(xs * spread(closing, 2 * j))
        state_out[tile] = dot(wh, bh, over) + (dot(wh, bl, over) + dot(wl, bh, over))


def tail_kernel(
    pos, tails, xh, bch, cum, dts, state, wx, bx, wbc, bbc,
    pay, x8_out, b8_out, c8_out, joined,
):
    even = pos[1] == 0
    wide = CH + 2 * ST
    joined[0:16, 0:CH] = tails[:, 0:CH].astype(f32)
    own, oth = tails[:, CH : CH + ST].astype(f32), tails[:, CH + ST :].astype(f32)
    joined[0:16, CH : CH + ST] = jnp.where(even, own, oth)
    joined[0:16, CH + ST :] = jnp.where(even, oth, own)
    joined[16:32, 0:CH] = xh[...]
    joined[16:32, CH:] = bch[...]
    taps, bias = taps_of(pos, wbc, bbc)
    b = conv(joined, slice(CH, CH + ST), taps[:, 0:ST], bias[:, 0:ST], 16, 8)
    c = conv(joined, slice(CH + ST, wide), taps[:, ST:], bias[:, ST:], 16, 8)
    b8_out[...] = b
    c8_out[...] = c
    x8 = conv(joined, slice(0, CH), wx[...], bx[...], 16, 8)
    x8_out[...] = x8
    last = cum[TOK - 1 : TOK]
    closing = jnp.exp(last - cum[0:8]) * dts[0:8]
    carry = jnp.exp(last)
    bh, bl = parts(b)
    over = ((0,), (0,))
    sub = lax.broadcasted_iota(jnp.int32, (16, ST), 0)
    for j in range(4):
        tile = slice(j * TILE, (j + 1) * TILE)
        wh, wl = parts(x8[:, tile] * spread(closing, 2 * j))
        full = state[tile] + (dot(wh, bh, over) + (dot(wh, bl, over) + dot(wl, bh, over)))
        for i in range(4):
            pay[4 * j + i, 0:32] = full[32 * i : 32 * i + 32].astype(bf16)
            head = 2 * j + i // 2
            value = jnp.broadcast_to(carry[:, head : head + 1], (16, ST))
            high = value.astype(bf16).astype(f32)
            pay[4 * j + i, 32:48] = jnp.where(sub == 0, high, value - high).astype(bf16)


def patched(first, rest):
    return jnp.concatenate([first, rest[8:]], axis=0)


def inner_kernel(xs, b, c, x8, b8, c8, cum, dts, z, sk, a_out, e_out, ch_out, cl_out):
    cc = patched(c8[...], c[...])
    ch, cl = parts(cc)
    ch_out[...] = ch
    cl_out[...] = cl
    bh, bl = parts(patched(b8[...], b[...]))
    over = ((1,), (1,))
    cb = dot(ch, bh, over) + (dot(ch, bl, over) + dot(cl, bh, over))
    cum_c = cum[...]
    cum_r = cum_c.T
    grow = jnp.exp(cum_c)
    dts_c = dts[...]
    row = lax.broadcasted_iota(jnp.int32, (TILE, TILE), 0)
    lane = lax.broadcasted_iota(jnp.int32, (TILE, TILE), 1)
    lower = row >= lane
    half = (slice(0, TILE), slice(TILE, TOK))
    for j in range(4):
        tile = slice(j * TILE, (j + 1) * TILE)
        x_tile = patched(x8[:, tile], xs[:, tile])
        x_dt = (x_tile * spread(dts_c, 2 * j)).astype(bf16)
        gate = silu(z[:, tile].astype(f32))
        grown = spread(grow, 2 * j)
        for i in range(2):
            ys = []
            for h in (2 * j, 2 * j + 1):
                cols = []
                for k in range(i + 1):
                    gap = cum_c[half[i], h : h + 1] - cum_r[h : h + 1, half[k]]
                    w = jnp.exp(jnp.minimum(gap, 0.0))
                    if k == i:
                        w = jnp.where(lower, w, 0.0)
                    cols.append((w * cb[half[i], half[k]]).astype(bf16))
                y = dot(cols[0], x_dt[half[0]], ((1,), (0,)))
                if i == 1:
                    y = y + dot(cols[1], x_dt[half[1]], ((1,), (0,)))
                ys.append(y)
            y = jnp.where(lane < 64, ys[0], ys[1])
            skip = jnp.where(lane[0:1] < 64, sk[:, 2 * j : 2 * j + 1], sk[:, 2 * j + 1 : 2 * j + 2])
            g = gate[half[i]]
            a_out[half[i], tile] = (y + skip * x_tile[half[i]]) * g
            e_out[half[i], tile] = grown[half[i]] * g


def scan_kernel(got, out):
    state = jnp.zeros((32, ST), f32)
    for k in range(16):
        out[k] = state.astype(bf16)
        if k < 15:
            carry = got[k, 32:33].astype(f32) + got[k, 33:34].astype(f32)
            state = carry * state + got[k, 0:32].astype(f32)


def pack(total):
    wide = jnp.concatenate([total, total], axis=1)
    high = wide.astype(bf16).astype(f32)
    lane = lax.broadcasted_iota(jnp.int32, (16, 2 * TOK), 1)
    sub = lax.broadcasted_iota(jnp.int32, (16, 2 * TOK), 0)
    value = jnp.where(lane < TOK, high, wide - high)
    return jnp.where(sub == 0, value, 0.0).astype(bf16)


def unpack(rows):
    wide = rows[0:1].astype(f32)
    return wide[:, 0:TOK] + wide[:, TOK:]


def gate_kernel(s, ch, cl, a, e, gain, h_out):
    ones = jnp.ones((8, TILE), f32)
    total = jnp.zeros((8, TOK), f32)
    over = ((1,), (1,))
    for j in range(4):
        tile = slice(j * TILE, (j + 1) * TILE)
        st = s[tile]
        carried = dot(ch[...], st, over) + dot(cl[...], st, over)
        gated = a[:, tile] + e[:, tile] * carried
        h_out[0:TOK, tile] = (gated * gain[:, tile]).astype(bf16)
        total = total + dot(ones, gated * gated, over, HIGH)
    h_out[TOK:] = pack(total[0:1])


def block(at, w, buf, sem, i):
    cols = pl.ds(pl.multiple_of(at * CH, CH), CH)
    return pltpu.make_async_copy(w.at[:, cols], buf, sem.at[i])


def fetch_kernel(at, w_own, w_oth, own_out, oth_out, sem):
    first = block(at[0], w_own, own_out, sem, 0)
    second = block(at[0], w_oth, oth_out, sem, 1)
    first.start()
    second.start()
    first.wait()
    second.wait()


def far_kernel(own, oth, w_own, w_oth, f_out, g_out):
    total = dot(own[0:TOK], w_own[...], ((1,), (0,))) + dot(oth[0:TOK], w_oth[...], ((1,), (0,)))
    f_out[0 : TOK // 2] = total[0 : TOK // 2].astype(bf16)
    f_out[TOK // 2 :] = pack(unpack(own[TOK:]) + unpack(oth[TOK:]))
    g_out[...] = total[TOK // 2 :].astype(bf16)


def near_kernel(count, at, own, oth, w_own, w_oth, *rest):
    outs, (buf, sem) = rest[:count], rest[count:]
    copies = []
    for i in range(count):
        for k, w in enumerate((w_own, w_oth)):
            copies.append(block(at[i], w, buf.at[2 * i + k], sem, 2 * i + k))
    for copy in copies:
        copy.start()
    for i in range(count):
        copies[2 * i].wait()
        copies[2 * i + 1].wait()
        total = dot(own[0:TOK], buf[2 * i], ((1,), (0,)))
        outs[i][...] = total + dot(oth[0:TOK], buf[2 * i + 1], ((1,), (0,)))


def first_kernel(rows, got, near, own, oth, out):
    base = rows[0]
    for i in (0, TOK // 2):
        part = near[i : i + TOK // 2]
        if i == base:
            part = part + got[0 : TOK // 2].astype(f32)
        out[i : i + TOK // 2] = part.astype(bf16)
    total = unpack(own[TOK:]) + unpack(oth[TOK:])
    if rows[1]:
        total = total + unpack(got[TOK // 2 :])
    out[TOK:] = pack(total)


def step_kernel(got, near, own, oth, out):
    out[0:TOK] = (near[...] + got[0:TOK].astype(f32)).astype(bf16)
    out[TOK:] = pack(unpack(own[TOK:]) + unpack(oth[TOK:]) + unpack(got[TOK:]))


def final_kernel(f, g, near, own, oth, out):
    total = unpack(own[TOK:]) + unpack(oth[TOK:]) + unpack(f[TOK:]) + unpack(g[TOK:])
    scale = lax.rsqrt(total / (NZ * 2 * CH) + 1e-05)
    scale = jnp.broadcast_to(scale, (8, TOK)).T[:, 0:1]
    summed = near[...] + f[0:TOK].astype(f32) + g[0:TOK].astype(f32)
    out[...] = (summed * scale).astype(bf16)


VM = pl.BlockSpec(memory_space=pltpu.VMEM)
SM = pl.BlockSpec(memory_space=pltpu.SMEM)
HB = pl.BlockSpec(memory_space=pl.ANY)


def near_by(value):
    return pltpu.with_memory_space_constraint(value, pltpu.VMEM)


def call(kernel, outs, ins, scratch=(), specs=None):
    specs = specs or "v" * len(ins)
    args, in_specs = [], []
    for kind, value in zip(specs, ins):
        args.append(near_by(value) if kind == "v" else value)
        in_specs.append({"v": VM, "s": SM, "h": HB, "p": VM}[kind])
    return pl.pallas_call(
        kernel,
        out_shape=[pltpu.VMEM(shape, kind) for shape, kind in outs],
        in_specs=in_specs,
        out_specs=[VM] * len(outs),
        scratch_shapes=list(scratch),
    )(*args)


def shards(x, z, bc, dt, decay_log, skip, conv_x, conv_bc, bias_x, bias_bc, gain, w):
    rank = lax.axis_index("tp")
    zi, ci = rank // 2, rank % 2
    pos = jnp.stack([zi, ci]).astype(jnp.int32)
    wide = CH + 2 * ST

    bo = other_core(bc)
    tails = next_block(jnp.concatenate([v[TOK - 16 :] for v in (x, bc, bo)], axis=1))
    weights = (conv_x, bias_x[None], conv_bc, bias_bc[None])
    xs, b, c, cum, dts, state, xh, bch = call(
        local_kernel,
        [
            ((TOK, CH), f32), ((TOK, ST), f32), ((TOK, ST), f32), ((TOK, HD), f32),
            ((TOK, HD), f32), ((CH, ST), f32), ((16, CH), f32), ((16, 2 * ST), f32),
        ],
        [pos, x, bc, bo, dt.T, decay_log[None], *weights],
        [pltpu.VMEM((TOK + 16, CH), f32), pltpu.VMEM((TOK + 16, 2 * ST), f32)],
        "sppvpppppp",
    )
    w_start, state = lax.optimization_barrier((w, state))
    w_other = other_core(w_start)
    pay, x8, b8, c8 = call(
        tail_kernel,
        [((16, 48, ST), bf16), ((8, CH), f32), ((8, ST), f32), ((8, ST), f32)],
        [pos, tails, xh, bch, cum, dts, state, *weights],
        [pltpu.VMEM((32, wide), f32)],
        "svvvvvvpppp",
    )
    got = lax.all_to_all(pay, "ctx", 0, 0, tiled=True)
    a, e, ch, cl = call(
        inner_kernel,
        [((TOK, CH), f32), ((TOK, CH), f32), ((TOK, ST), bf16), ((TOK, ST), bf16)],
        [xs, b, c, x8, b8, c8, cum, dts, z, skip[None]],
        (),
        "vvvvvvvvpp",
    )
    got, a = lax.optimization_barrier((got, a))
    (back,) = call(scan_kernel, [((16, 32, ST), bf16)], [got])
    incoming = lax.all_to_all(back, "ctx", 0, 0, tiled=True).reshape(CH, ST)

    def column(d):
        return ((zi + d) % NZ) * 2 + ci

    def columns(*ds):
        return jnp.stack([column(d) for d in ds]).astype(jnp.int32)

    far_own, far_oth = call(
        fetch_kernel,
        [((CH, CH), bf16)] * 2,
        [columns(4), w, w_other],
        [pltpu.SemaphoreType.DMA((2,))],
        "shh",
    )
    (hidden,) = call(
        gate_kernel,
        [((TOK + 16, CH), bf16)],
        [incoming, ch, cl, a, e, gain[None]],
        (),
        "vvvvvp",
    )
    hidden_o = other_core(hidden)
    pair = (hidden, hidden_o)

    def near(*ds):
        n = len(ds)
        return call(
            partial(near_kernel, n),
            [((TOK, CH), f32)] * n,
            [columns(*ds), *pair, w, w_other],
            [pltpu.VMEM((2 * n, CH, CH), bf16), pltpu.SemaphoreType.DMA((2 * n,))],
            "svvhh",
        )

    half = TOK // 2
    f, g = call(far_kernel, [((half + 16, CH), bf16), ((half, CH), bf16)], [*pair, far_own, far_oth])
    f, g = up(f), down(g)
    nf, ng = near(3, 5)
    sent = [((TOK + 16, CH), bf16)]
    (f,) = call(partial(first_kernel, (0, True)), sent, [f, nf, *pair])
    (g,) = call(partial(first_kernel, (half, False)), sent, [g, ng, *pair])
    for d in (2, 1):
        f, g = up(f), down(g)
        nf, ng = near(d, 8 - d)
        (f,) = call(step_kernel, sent, [f, nf, *pair])
        (g,) = call(step_kernel, sent, [g, ng, *pair])
    f, g = up(f), down(g)
    (own,) = near(0)
    return pl.pallas_call(
        final_kernel,
        out_shape=jax.ShapeDtypeStruct((TOK, CH), bf16),
        in_specs=[VM] * 5,
        out_specs=VM,
    )(*[near_by(v) for v in (f, g, own, *pair)])


def solution(mesh):
    return jax.shard_map(
        shards,
        mesh=mesh,
        in_specs=(
            P("ctx", "tp"),
            P("ctx", "tp"),
            P("ctx", "tp"),
            P("ctx", "tp"),
            P("tp"),
            P("tp"),
            P(None, "tp"),
            P(),
            P("tp"),
            P(),
            P("tp"),
            P("tp", None),
        ),
        out_specs=P("ctx", "tp"),
        check_vma=False,
    )
```

```python
from functools import partial

import jax
import jax.numpy as jnp
from jax import lax
from jax.experimental import pallas as pl
from jax.experimental.pallas import tpu as pltpu
from jax.sharding import PartitionSpec as P


bf16 = jnp.bfloat16
f32 = jnp.float32
HIGH = lax.Precision.HIGHEST
AXES = ("ctx", "tp")
NX, NY, NZ = 4, 4, 8
TOK = 256
CH = 512
HD = 8
ST = 128
TILE = 128
SPLIT = 2
WQ = 2 * CH // SPLIT


def permute(value, target):
    pairs = []
    for ctx in range(NX * NY):
        for z in range(NZ):
            for c in range(2):
                to = target(ctx, z, c)
                if to is not None:
                    pairs.append((ctx * 16 + z * 2 + c, to[0] * 16 + (to[1] % NZ) * 2 + to[2]))
    return lax.ppermute(value, AXES, pairs)


def next_block(value):
    return permute(value, lambda k, z, c: (k + 1, z, c) if k < 15 else None)


def other_core(value):
    return permute(value, lambda k, z, c: (k, z, 1 - c))


def onward(value):
    return permute(value, lambda k, z, c: (k, z + 1 - 2 * c, c))


def place():
    rank = lax.axis_index("tp")
    return rank // 2, rank % 2


def silu(v):
    return v / (1.0 + jnp.exp(-v))


def dot(a, b, dims, precision=None):
    return lax.dot_general(a, b, (dims, ((), ())), precision=precision, preferred_element_type=f32)


def parts(v):
    high = v.astype(bf16)
    return high, (v - high.astype(f32)).astype(bf16)


def spread(cols, first):
    lane = lax.broadcasted_iota(jnp.int32, (cols.shape[0], TILE), 1)
    return jnp.where(lane < 64, cols[:, first : first + 1], cols[:, first + 1 : first + 2])


def conv(ref, tile, taps, bias, first, rows):
    total = bias
    for k in range(4):
        total = total + taps[k : k + 1] * ref[first - 3 + k : first - 3 + k + rows, tile]
    return silu(total)


def pack_tails_kernel(x, bc, bo, out, sem):
    rows = slice(TOK - 16, TOK)
    first = pltpu.make_async_copy(x.at[rows], out.at[:, 0:CH], sem.at[0])
    second = pltpu.make_async_copy(bc.at[rows], out.at[:, CH : CH + ST], sem.at[1])
    first.start()
    second.start()
    out[:, CH + ST :] = bo[rows]
    first.wait()
    second.wait()


def local_kernel(
    x, bc, bo, dt_t, dl, wx, bx, wbc, bbc,
    xs_out, b_out, c_out, cum_out, dts_out, state_out, xh_out, bch_out, w_out, bias_out,
    joined, joined_bc,
):
    zi, ci = place()
    even = ci == 0
    joined[0:16] = jnp.zeros((16, CH), f32)
    joined[16:] = x[...].astype(f32)
    own, oth = bc[...].astype(f32), bo[...].astype(f32)
    joined_bc[0:16] = jnp.zeros((16, 2 * ST), f32)
    joined_bc[16:, 0:ST] = jnp.where(even, own, oth)
    joined_bc[16:, ST:] = jnp.where(even, oth, own)
    xh_out[...] = joined[16:32]
    bch_out[...] = joined_bc[16:32]
    group = pl.ds(pl.multiple_of(zi * 2 * ST, 2 * ST), 2 * ST)
    taps, bias = wbc[:, group], bbc[:, group]
    w_out[:, 0:CH] = wx[...]
    w_out[:, CH:] = taps
    bias_out[:, 0:CH] = bx[...]
    bias_out[:, CH:] = bias
    b = conv(joined_bc, slice(0, ST), taps[:, 0:ST], bias[:, 0:ST], 16, TOK)
    c = conv(joined_bc, slice(ST, 2 * ST), taps[:, ST:], bias[:, ST:], 16, TOK)
    b_out[...] = b
    c_out[...] = c
    dts = jnp.logaddexp(dt_t[...], 0.0).T
    dts_out[...] = dts
    row = lax.broadcasted_iota(jnp.int32, (TOK, TOK), 0)
    col = lax.broadcasted_iota(jnp.int32, (TOK, TOK), 1)
    cum = dot((row >= col).astype(f32), dts * -jnp.exp(dl[...]), ((1,), (0,)), HIGH)
    cum_out[...] = cum
    closing = jnp.exp(cum[TOK - 1 : TOK] - cum) * dts
    late = lax.broadcasted_iota(jnp.int32, (TOK, HD), 0) >= 8
    closing = jnp.where(late, closing, 0.0)
    bh, bl = parts(b)
    over = ((0,), (0,))
    for j in range(4):
        tile = slice(j * TILE, (j + 1) * TILE)
        xs = conv(joined, tile, wx[:, tile], bx[:, tile], 16, TOK)
        xs_out[:, tile] = xs
        wh, wl = parts(xs * spread(closing, 2 * j))
        state_out[tile] = dot(wh, bh, over) + (dot(wh, bl, over) + dot(wl, bh, over))


def tail_kernel(tails, xh, bch, cum, dts, state, w, bias, pay, first_out, joined):
    even = place()[1] == 0
    joined[0:16, 0:CH] = tails[:, 0:CH].astype(f32)
    own, oth = tails[:, CH : CH + ST].astype(f32), tails[:, CH + ST :].astype(f32)
    joined[0:16, CH : CH + ST] = jnp.where(even, own, oth)
    joined[0:16, CH + ST :] = jnp.where(even, oth, own)
    joined[16:32, 0:CH] = xh[...]
    joined[16:32, CH:] = bch[...]
    rows = conv(joined, slice(0, CH + 2 * ST), w[...], bias[...], 16, 8)
    first_out[...] = rows
    last = cum[TOK - 1 : TOK]
    closing = jnp.exp(last - cum[0:8]) * dts[0:8]
    carry = jnp.exp(last)
    bh, bl = parts(rows[:, CH : CH + ST])
    over = ((0,), (0,))
    sub = lax.broadcasted_iota(jnp.int32, (16, ST), 0)
    for j in range(4):
        tile = slice(j * TILE, (j + 1) * TILE)
        wh, wl = parts(rows[:, tile] * spread(closing, 2 * j))
        full = state[tile] + (dot(wh, bh, over) + (dot(wh, bl, over) + dot(wl, bh, over)))
        for i in range(4):
            pay[4 * j + i, 0:32] = full[32 * i : 32 * i + 32].astype(bf16)
            if i % 2 == 0:
                head = 2 * j + i // 2
                value = jnp.broadcast_to(carry[:, head : head + 1], (16, ST))
                high = value.astype(bf16).astype(f32)
                both = jnp.where(sub == 0, high, value - high).astype(bf16)
            pay[4 * j + i, 32:48] = both


def patched(first, rest):
    return jnp.concatenate([first, rest[8:]], axis=0)


def inner_kernel(xs, b, c, first, cum, dts, z, sk, gain, a_out, e_out, ch_out, cl_out, gain_out):
    gain_out[...] = gain[...]
    cc = patched(first[:, CH + ST :], c[...])
    ch, cl = parts(cc)
    ch_out[...] = ch
    cl_out[...] = cl
    bh, bl = parts(patched(first[:, CH : CH + ST], b[...]))
    over = ((1,), (1,))
    cb = dot(ch, bh, over) + (dot(ch, bl, over) + dot(cl, bh, over))
    cum_c = cum[...]
    cum_r = cum_c.T
    grow = jnp.exp(cum_c)
    dts_c = dts[...]
    row = lax.broadcasted_iota(jnp.int32, (TILE, TILE), 0)
    lane = lax.broadcasted_iota(jnp.int32, (TILE, TILE), 1)
    lower = row >= lane
    half = (slice(0, TILE), slice(TILE, TOK))
    for j in range(4):
        tile = slice(j * TILE, (j + 1) * TILE)
        x_tile = patched(first[:, tile], xs[:, tile])
        x_dt = (x_tile * spread(dts_c, 2 * j)).astype(bf16)
        gate = silu(z[:, tile].astype(f32))
        grown = spread(grow, 2 * j)
        for i in range(2):
            ys = []
            for h in (2 * j, 2 * j + 1):
                cols = []
                for k in range(i + 1):
                    gap = cum_c[half[i], h : h + 1] - cum_r[h : h + 1, half[k]]
                    w = jnp.exp(jnp.minimum(gap, 0.0))
                    if k == i:
                        w = jnp.where(lower, w, 0.0)
                    cols.append((w * cb[half[i], half[k]]).astype(bf16))
                y = dot(cols[0], x_dt[half[0]], ((1,), (0,)))
                if i == 1:
                    y = y + dot(cols[1], x_dt[half[1]], ((1,), (0,)))
                ys.append(y)
            y = jnp.where(lane < 64, ys[0], ys[1])
            skip = jnp.where(lane[0:1] < 64, sk[:, 2 * j : 2 * j + 1], sk[:, 2 * j + 1 : 2 * j + 2])
            g = gate[half[i]]
            a_out[half[i], tile] = (y + skip * x_tile[half[i]]) * g
            e_out[half[i], tile] = grown[half[i]] * g


def scan_kernel(got, out):
    state = jnp.zeros((32, ST), f32)
    for k in range(16):
        out[k] = state.astype(bf16)
        if k < 15:
            carry = got[k, 32:33].astype(f32) + got[k, 33:34].astype(f32)
            state = carry * state + got[k, 0:32].astype(f32)


def pack(total):
    high = total.astype(bf16).astype(f32)
    sub = lax.broadcasted_iota(jnp.int32, (16, TOK), 0)
    value = jnp.where(sub == 0, high, total - high)
    return jnp.where(sub < 2, value, 0.0).astype(bf16)


def unpack(ref, first=TOK):
    rows = ref[first : first + 16, 0:TOK].astype(f32)
    return rows[0:1] + rows[1:2]


def gate_kernel(s, ch, cl, a, e, gain, h_out):
    total = jnp.zeros((TOK, TILE), f32)
    over = ((1,), (1,))
    for j in range(4):
        tile = slice(j * TILE, (j + 1) * TILE)
        st = s[tile]
        carried = dot(ch[...], st, over) + dot(cl[...], st, over)
        gated = a[:, tile] + e[:, tile] * carried
        h_out[0:TOK, tile] = (gated * gain[:, tile]).astype(bf16)
        total = total + gated * gated
    h_out[TOK:, 0:TOK] = pack(jnp.sum(total.T, axis=0, keepdims=True))
    h_out[TOK:, TOK:] = jnp.zeros((16, CH - TOK), bf16)


def chip_block(d, w, buf, sem):
    zi, ci = place()
    at = (zi + d * (1 - 2 * ci)) & (NZ - 1)
    cols = pl.ds(pl.multiple_of(at * 2 * CH, 2 * CH), 2 * CH)
    return pltpu.make_async_copy(w.at[:, cols], buf, sem)


def fetch_kernel(w_own, w_oth, own_out, oth_out, sem):
    first = chip_block(4, w_own, own_out, sem.at[0])
    second = chip_block(4, w_oth, oth_out, sem.at[1])
    first.start()
    second.start()
    first.wait()
    second.wait()


def stream(q):
    side = (q * WQ) // CH
    ci = place()[1]
    return pl.ds(pl.multiple_of((ci ^ 1 ^ side) * CH + (q * WQ) % CH, WQ), WQ)


def far_kernel(own, oth, w_own, w_oth, *outs):
    ci = place()[1]
    rows = pl.ds(pl.multiple_of(ci * (TOK // 2), TOK // 2), TOK // 2)
    lhs, lhs_o = own[rows], oth[rows]
    for q in range(SPLIT):
        at = stream(q)
        total = dot(lhs, w_own[:, at], ((1,), (0,))) + dot(lhs_o, w_oth[:, at], ((1,), (0,)))
        outs[q][0 : TOK // 2] = total.astype(bf16)
    squares = jnp.where(ci == 0, unpack(own) + unpack(oth), 0.0)
    put_squares(outs[0], TOK // 2, squares)


def put_squares(out, first, squares):
    out[first:, 0:TOK] = pack(squares)
    if WQ > TOK:
        out[first:, TOK:] = jnp.zeros((16, WQ - TOK), bf16)


def near_kernel(d, own, oth, w_own, w_oth, *rest):
    outs, (buf, buf_o, sem) = rest[:SPLIT], rest[SPLIT:]
    first = chip_block(d, w_own, buf, sem.at[0])
    second = chip_block(d, w_oth, buf_o, sem.at[1])
    first.start()
    second.start()
    first.wait()
    second.wait()
    lhs, lhs_o = own[0:TOK], oth[0:TOK]
    for q in range(SPLIT):
        at = stream(q)
        outs[q][...] = dot(lhs, buf[:, at], ((1,), (0,))) + dot(lhs_o, buf_o[:, at], ((1,), (0,)))


def home_kernel(own, oth, w_own, w_oth, out, buf, buf_o, sem):
    zi, ci = place()
    cols = pl.ds(pl.multiple_of((zi * 2 + ci) * CH, CH), CH)
    first = pltpu.make_async_copy(w_own.at[:, cols], buf, sem.at[0])
    second = pltpu.make_async_copy(w_oth.at[:, cols], buf_o, sem.at[1])
    first.start()
    second.start()
    first.wait()
    second.wait()
    total = dot(own[0:TOK], buf[...], ((1,), (0,)))
    out[...] = total + dot(oth[0:TOK], buf_o[...], ((1,), (0,)))


def first_kernel(q, got, near, *rest):
    out = rest[-1]
    half = TOK // 2
    ci = place()[1]
    hit = pl.ds(pl.multiple_of(ci * half, half), half)
    rest_rows = pl.ds(pl.multiple_of((1 - ci) * half, half), half)
    out[hit] = (near[hit] + got[0:half].astype(f32)).astype(bf16)
    out[rest_rows] = near[rest_rows].astype(bf16)
    if q == 0:
        own, oth = rest[:2]
        put_squares(out, TOK, unpack(own) + unpack(oth) + unpack(got, half))


def step_kernel(q, got, near, *rest):
    out = rest[-1]
    out[0:TOK] = (near[...] + got[0:TOK].astype(f32)).astype(bf16)
    if q == 0:
        own, oth = rest[:2]
        put_squares(out, TOK, unpack(own) + unpack(oth) + unpack(got))


def final_kernel(own, oth, home, mine, *rest):
    out = rest[-1]
    n = SPLIT // 2
    swapped, kept = rest[:n], rest[n : 2 * n]
    total = unpack(own) + unpack(oth) + unpack(mine) + unpack(swapped[0])
    scale = lax.rsqrt(total / (NZ * 2 * CH) + 1e-05)
    scale = jnp.broadcast_to(scale, (8, TOK)).T[:, 0:1]
    for q in range(n):
        tile = slice(q * WQ, (q + 1) * WQ)
        summed = home[:, tile] + kept[q][0:TOK].astype(f32) + swapped[q][0:TOK].astype(f32)
        out[:, tile] = (summed * scale).astype(bf16)


VM = pl.BlockSpec(memory_space=pltpu.VMEM)
SPACE = {"v": pltpu.VMEM, "p": pltpu.HBM, "h": pltpu.HBM}
SMALL = pltpu.CompilerParams(vmem_limit_bytes=12 * 2**20)
HB = pl.BlockSpec(memory_space=pltpu.HBM)


def near_by(value):
    return pltpu.with_memory_space_constraint(value, pltpu.VMEM)


def call(kernel, outs, ins, scratch=(), specs=None):
    specs = specs or "v" * len(ins)
    args, in_specs = [], []
    for kind, value in zip(specs, ins):
        args.append(pltpu.with_memory_space_constraint(value, SPACE[kind]))
        in_specs.append({"v": VM, "h": HB, "p": VM}[kind])
    return pl.pallas_call(
        kernel,
        out_shape=[pltpu.VMEM(shape, kind) for shape, kind in outs],
        in_specs=in_specs,
        out_specs=[VM] * len(outs),
        scratch_shapes=list(scratch),
        compiler_params=SMALL,
    )(*args)


def shards(x, z, bc, dt, decay_log, skip, conv_x, conv_bc, bias_x, bias_bc, gain, w):
    wide = CH + 2 * ST
    half = TOK // 2

    bo = other_core(bc)
    (tails,) = call(
        pack_tails_kernel,
        [((16, wide), bf16)],
        [x, bc, bo],
        [pltpu.SemaphoreType.DMA((2,))],
        "hhv",
    )
    tails = next_block(tails)
    xs, b, c, cum, dts, state, xh, bch, taps, bias = call(
        local_kernel,
        [
            ((TOK, CH), f32), ((TOK, ST), f32), ((TOK, ST), f32), ((TOK, HD), f32),
            ((TOK, HD), f32), ((CH, ST), f32), ((16, CH), f32), ((16, 2 * ST), f32),
            ((4, wide), f32), ((1, wide), f32),
        ],
        [x, bc, bo, dt.T, decay_log[None], conv_x, bias_x[None], conv_bc, bias_bc[None]],
        [pltpu.VMEM((TOK + 16, CH), f32), pltpu.VMEM((TOK + 16, 2 * ST), f32)],
        "ppvpppppp",
    )
    w_other = other_core(w)
    pay, first = call(
        tail_kernel,
        [((16, 48, ST), bf16), ((8, wide), f32)],
        [tails, xh, bch, cum, dts, state, taps, bias],
        [pltpu.VMEM((32, wide), f32)],
    )
    got = lax.all_to_all(pay, "ctx", 0, 0, tiled=True)
    a, e, ch, cl, gains = call(
        inner_kernel,
        [((TOK, CH), f32), ((TOK, CH), f32), ((TOK, ST), bf16), ((TOK, ST), bf16), ((1, CH), f32)],
        [xs, b, c, first, cum, dts, z, skip[None], gain[None]],
        (),
        "vvvvvvppp",
    )
    (back,) = call(scan_kernel, [((16, 32, ST), bf16)], [got])
    incoming = lax.all_to_all(back, "ctx", 0, 0, tiled=True)
    incoming = incoming.reshape(CH, ST)
    copies = [pltpu.SemaphoreType.DMA((2,))]
    far = call(fetch_kernel, [((CH, 2 * CH), bf16)] * 2, [w, w_other], copies, "hh")
    (hidden,) = call(gate_kernel, [((TOK + 16, CH), bf16)], [incoming, ch, cl, a, e, gains])
    pair = (hidden, other_core(hidden))

    def near(d):
        return call(
            partial(near_kernel, d),
            [((TOK, WQ), f32)] * SPLIT,
            [*pair, w, w_other],
            [pltpu.VMEM((CH, 2 * CH), bf16)] * 2 + copies,
            "vvhh",
        )

    def extra(rows, q):
        return ((rows + 16 if q == 0 else rows, WQ), bf16)

    def add(kernel, q, got, part):
        more = pair if q == 0 else ()
        return call(partial(kernel, q), [extra(TOK, q)], [got, part, *more])[0]

    sums = call(far_kernel, [extra(half, q) for q in range(SPLIT)], [*pair, *far])

    def hop():
        out = []
        for q in range(SPLIT):
            out.append(onward(sums[q]))
        return out

    for d in (3, 2, 1):
        sums = hop()
        part = near(d)
        kernel = first_kernel if d == 3 else step_kernel
        sums = [add(kernel, q, sums[q], part[q]) for q in range(SPLIT)]
    sums = hop()
    (home,) = call(
        home_kernel,
        [((TOK, CH), f32)],
        [*pair, w, w_other],
        [pltpu.VMEM((CH, CH), bf16)] * 2 + copies,
        "vvhh",
    )
    n = SPLIT // 2
    swapped = []
    for q in range(n):
        swapped.append(other_core(sums[q]))
    ins = [*pair, home, sums[0], *swapped, *sums[n:]]
    return pl.pallas_call(
        final_kernel,
        out_shape=jax.ShapeDtypeStruct((TOK, CH), bf16),
        in_specs=[VM] * len(ins),
        out_specs=VM,
        compiler_params=SMALL,
    )(*[near_by(v) for v in ins])


def solution(mesh):
    return jax.shard_map(
        shards,
        mesh=mesh,
        in_specs=(
            P("ctx", "tp"),
            P("ctx", "tp"),
            P("ctx", "tp"),
            P("ctx", "tp"),
            P("tp"),
            P("tp"),
            P(None, "tp"),
            P(),
            P("tp"),
            P(),
            P("tp"),
            P("tp", None),
        ),
        out_specs=P("ctx", "tp"),
        check_vma=False,
    )
```

```python
from functools import partial

import jax
import jax.numpy as jnp
from jax import lax
from jax.experimental import pallas as pl
from jax.experimental.pallas import tpu as pltpu
from jax.sharding import PartitionSpec as P


bf16 = jnp.bfloat16
f32 = jnp.float32
HIGH = lax.Precision.HIGHEST
AXES = ("ctx", "tp")
NX, NY, NZ = 4, 4, 8
TOK = 256
CH = 512
HD = 8
ST = 128
TILE = 128
SPLIT = 2
WQ = 2 * CH // SPLIT


def permute(value, target):
    pairs = []
    for ctx in range(NX * NY):
        for z in range(NZ):
            for c in range(2):
                to = target(ctx, z, c)
                if to is not None:
                    pairs.append((ctx * 16 + z * 2 + c, to[0] * 16 + (to[1] % NZ) * 2 + to[2]))
    return lax.ppermute(value, AXES, pairs)


def next_block(value):
    return permute(value, lambda k, z, c: (k + 1, z, c) if k < 15 else None)


def other_core(value):
    return permute(value, lambda k, z, c: (k, z, 1 - c))


def onward(value):
    return permute(value, lambda k, z, c: (k, z + 1 - 2 * c, c))


def place():
    rank = lax.axis_index("tp")
    return rank // 2, rank % 2


def silu(v):
    return v / (1.0 + jnp.exp(-v))


def dot(a, b, dims, precision=None):
    return lax.dot_general(a, b, (dims, ((), ())), precision=precision, preferred_element_type=f32)


def parts(v):
    high = v.astype(bf16)
    return high, (v - high.astype(f32)).astype(bf16)


def spread(cols, first):
    lane = lax.broadcasted_iota(jnp.int32, (cols.shape[0], TILE), 1)
    return jnp.where(lane < 64, cols[:, first : first + 1], cols[:, first + 1 : first + 2])


def conv(ref, tile, taps, bias, first, rows):
    total = bias
    for k in range(4):
        total = total + taps[k : k + 1] * ref[first - 3 + k : first - 3 + k + rows, tile]
    return silu(total)


def load_kernel(*refs):
    n = len(refs) // 2
    sem = refs[-1]
    copies = [pltpu.make_async_copy(refs[i], refs[n + i], sem.at[i]) for i in range(n)]
    for copy in copies:
        copy.start()
    for copy in copies:
        copy.wait()


def pack_tails_kernel(x, bc, bo, out):
    rows = slice(TOK - 16, TOK)
    out[:, 0:CH] = x[rows]
    out[:, CH : CH + ST] = bc[rows]
    out[:, CH + ST :] = bo[rows]


def local_kernel(
    x, bc, bo, dt_t, dl, wx, bx, wbc, bbc,
    xs_out, b_out, c_out, cum_out, dts_out, state_out, xh_out, bch_out, w_out, bias_out,
    joined, joined_bc,
):
    zi, ci = place()
    even = ci == 0
    joined[0:16] = jnp.zeros((16, CH), f32)
    joined[16:] = x[...].astype(f32)
    own, oth = bc[...].astype(f32), bo[...].astype(f32)
    joined_bc[0:16] = jnp.zeros((16, 2 * ST), f32)
    joined_bc[16:, 0:ST] = jnp.where(even, own, oth)
    joined_bc[16:, ST:] = jnp.where(even, oth, own)
    xh_out[...] = joined[16:32]
    bch_out[...] = joined_bc[16:32]
    group = pl.ds(pl.multiple_of(zi * 2 * ST, 2 * ST), 2 * ST)
    taps, bias = wbc[:, group], bbc[:, group]
    w_out[:, 0:CH] = wx[...]
    w_out[:, CH:] = taps
    bias_out[:, 0:CH] = bx[...]
    bias_out[:, CH:] = bias
    b = conv(joined_bc, slice(0, ST), taps[:, 0:ST], bias[:, 0:ST], 16, TOK)
    c = conv(joined_bc, slice(ST, 2 * ST), taps[:, ST:], bias[:, ST:], 16, TOK)
    b_out[...] = b
    c_out[...] = c
    dts = jnp.logaddexp(dt_t[...], 0.0).T
    dts_out[...] = dts
    row = lax.broadcasted_iota(jnp.int32, (TOK, TOK), 0)
    col = lax.broadcasted_iota(jnp.int32, (TOK, TOK), 1)
    cum = dot((row >= col).astype(f32), dts * -jnp.exp(dl[...]), ((1,), (0,)), HIGH)
    cum_out[...] = cum
    closing = jnp.exp(cum[TOK - 1 : TOK] - cum) * dts
    late = lax.broadcasted_iota(jnp.int32, (TOK, HD), 0) >= 8
    closing = jnp.where(late, closing, 0.0)
    bh, bl = parts(b)
    over = ((0,), (0,))
    for j in range(4):
        tile = slice(j * TILE, (j + 1) * TILE)
        xs = conv(joined, tile, wx[:, tile], bx[:, tile], 16, TOK)
        xs_out[:, tile] = xs
        wh, wl = parts(xs * spread(closing, 2 * j))
        state_out[tile] = dot(wh, bh, over) + (dot(wh, bl, over) + dot(wl, bh, over))


def tail_kernel(tails, xh, bch, cum, dts, state, w, bias, pay, first_out, joined):
    even = place()[1] == 0
    joined[0:16, 0:CH] = tails[:, 0:CH].astype(f32)
    own, oth = tails[:, CH : CH + ST].astype(f32), tails[:, CH + ST :].astype(f32)
    joined[0:16, CH : CH + ST] = jnp.where(even, own, oth)
    joined[0:16, CH + ST :] = jnp.where(even, oth, own)
    joined[16:32, 0:CH] = xh[...]
    joined[16:32, CH:] = bch[...]
    rows = conv(joined, slice(0, CH + 2 * ST), w[...], bias[...], 16, 8)
    first_out[...] = rows
    last = cum[TOK - 1 : TOK]
    closing = jnp.exp(last - cum[0:8]) * dts[0:8]
    carry = jnp.exp(last)
    b = rows[:, CH : CH + ST]
    b_high = b.astype(bf16).astype(f32)
    none = jnp.zeros((8, ST), f32)
    stacked_b = jnp.concatenate([b_high, b_high, b - b_high, none], axis=0).astype(bf16)
    over = ((0,), (0,))
    sub = lax.broadcasted_iota(jnp.int32, (16, ST), 0)
    for j in range(4):
        tile = slice(j * TILE, (j + 1) * TILE)
        v = rows[:, tile] * spread(closing, 2 * j)
        v_high = v.astype(bf16).astype(f32)
        stacked = jnp.concatenate([v_high, v - v_high, v_high, none], axis=0).astype(bf16)
        full = state[tile] + dot(stacked, stacked_b, over)
        for i in range(4):
            pay[4 * j + i, 0:32] = full[32 * i : 32 * i + 32].astype(bf16)
            if i % 2 == 0:
                head = 2 * j + i // 2
                value = jnp.broadcast_to(carry[:, head : head + 1], (16, ST))
                high = value.astype(bf16).astype(f32)
                both = jnp.where(sub == 0, high, value - high).astype(bf16)
            pay[4 * j + i, 32:48] = both


def patched(first, rest):
    return jnp.concatenate([first, rest[8:]], axis=0)


def inner_kernel(xs, b, c, first, cum, dts, z, sk, gain, a_out, e_out, ch_out, cl_out, gain_out):
    gain_out[...] = gain[...]
    cc = patched(first[:, CH + ST :], c[...])
    ch, cl = parts(cc)
    ch_out[...] = ch
    cl_out[...] = cl
    bh, bl = parts(patched(first[:, CH : CH + ST], b[...]))
    over = ((1,), (1,))
    cb = dot(ch, bh, over) + (dot(ch, bl, over) + dot(cl, bh, over))
    cum_c = cum[...]
    cum_r = cum_c.T
    grow = jnp.exp(cum_c)
    dts_c = dts[...]
    row = lax.broadcasted_iota(jnp.int32, (TILE, TILE), 0)
    lane = lax.broadcasted_iota(jnp.int32, (TILE, TILE), 1)
    lower = row >= lane
    half = (slice(0, TILE), slice(TILE, TOK))
    for j in range(4):
        tile = slice(j * TILE, (j + 1) * TILE)
        x_tile = patched(first[:, tile], xs[:, tile])
        x_dt = (x_tile * spread(dts_c, 2 * j)).astype(bf16)
        gate = silu(z[:, tile].astype(f32))
        grown = spread(grow, 2 * j)
        for i in range(2):
            ys = []
            for h in (2 * j, 2 * j + 1):
                cols = []
                for k in range(i + 1):
                    gap = cum_c[half[i], h : h + 1] - cum_r[h : h + 1, half[k]]
                    w = jnp.exp(jnp.minimum(gap, 0.0))
                    if k == i:
                        w = jnp.where(lower, w, 0.0)
                    cols.append((w * cb[half[i], half[k]]).astype(bf16))
                y = dot(cols[0], x_dt[half[0]], ((1,), (0,)))
                if i == 1:
                    y = y + dot(cols[1], x_dt[half[1]], ((1,), (0,)))
                ys.append(y)
            y = jnp.where(lane < 64, ys[0], ys[1])
            skip = jnp.where(lane[0:1] < 64, sk[:, 2 * j : 2 * j + 1], sk[:, 2 * j + 1 : 2 * j + 2])
            g = gate[half[i]]
            a_out[half[i], tile] = (y + skip * x_tile[half[i]]) * g
            e_out[half[i], tile] = grown[half[i]] * g


def scan_kernel(got, out):
    state = jnp.zeros((32, ST), f32)
    for k in range(16):
        out[k] = state.astype(bf16)
        if k < 15:
            carry = got[k, 32:33].astype(f32) + got[k, 33:34].astype(f32)
            state = carry * state + got[k, 0:32].astype(f32)


def pack(total):
    high = total.astype(bf16).astype(f32)
    sub = lax.broadcasted_iota(jnp.int32, (16, TOK), 0)
    value = jnp.where(sub == 0, high, total - high)
    return jnp.where(sub < 2, value, 0.0).astype(bf16)


def unpack(ref, first=TOK):
    rows = ref[first : first + 16, 0:TOK].astype(f32)
    return rows[0:1] + rows[1:2]


def gate_kernel(s, ch, cl, a, e, gain, h_out):
    total = jnp.zeros((TOK, TILE), f32)
    over = ((1,), (1,))
    for j in range(4):
        tile = slice(j * TILE, (j + 1) * TILE)
        st = s[tile]
        carried = dot(ch[...], st, over) + dot(cl[...], st, over)
        gated = a[:, tile] + e[:, tile] * carried
        h_out[0:TOK, tile] = (gated * gain[:, tile]).astype(bf16)
        total = total + gated * gated
    h_out[TOK:, 0:TOK] = pack(jnp.sum(total.T, axis=0, keepdims=True))
    h_out[TOK:, TOK:] = jnp.zeros((16, CH - TOK), bf16)


def chip_block(d, w, buf, sem):
    zi, ci = place()
    at = (zi + d * (1 - 2 * ci)) & (NZ - 1)
    cols = pl.ds(pl.multiple_of(at * 2 * CH, 2 * CH), 2 * CH)
    return pltpu.make_async_copy(w.at[:, cols], buf, sem)


def fetch_kernel(w_own, w_oth, own_out, oth_out, sem):
    first = chip_block(4, w_own, own_out, sem.at[0])
    second = chip_block(4, w_oth, oth_out, sem.at[1])
    first.start()
    second.start()
    first.wait()
    second.wait()


def stream(q):
    side = (q * WQ) // CH
    ci = place()[1]
    return pl.ds(pl.multiple_of((ci ^ 1 ^ side) * CH + (q * WQ) % CH, WQ), WQ)


def far_kernel(own, oth, w_own, w_oth, *outs):
    ci = place()[1]
    rows = pl.ds(pl.multiple_of(ci * (TOK // 2), TOK // 2), TOK // 2)
    lhs, lhs_o = own[rows], oth[rows]
    for q in range(SPLIT):
        at = stream(q)
        total = dot(lhs, w_own[:, at], ((1,), (0,))) + dot(lhs_o, w_oth[:, at], ((1,), (0,)))
        outs[q][0 : TOK // 2] = total.astype(bf16)
    squares = jnp.where(ci == 0, unpack(own) + unpack(oth), 0.0)
    put_squares(outs[0], TOK // 2, squares)


def put_squares(out, first, squares):
    out[first:, 0:TOK] = pack(squares)
    if WQ > TOK:
        out[first:, TOK:] = jnp.zeros((16, WQ - TOK), bf16)


def near_kernel(d, own, oth, w_own, w_oth, *rest):
    outs, (buf, buf_o, sem) = rest[:SPLIT], rest[SPLIT:]
    first = chip_block(d, w_own, buf, sem.at[0])
    second = chip_block(d, w_oth, buf_o, sem.at[1])
    first.start()
    second.start()
    first.wait()
    second.wait()
    lhs, lhs_o = own[0:TOK], oth[0:TOK]
    for q in range(SPLIT):
        at = stream(q)
        outs[q][...] = dot(lhs, buf[:, at], ((1,), (0,))) + dot(lhs_o, buf_o[:, at], ((1,), (0,)))


def home_kernel(own, oth, w_own, w_oth, out, buf, buf_o, sem):
    zi, ci = place()
    cols = pl.ds(pl.multiple_of((zi * 2 + ci) * CH, CH), CH)
    first = pltpu.make_async_copy(w_own.at[:, cols], buf, sem.at[0])
    second = pltpu.make_async_copy(w_oth.at[:, cols], buf_o, sem.at[1])
    first.start()
    second.start()
    first.wait()
    second.wait()
    total = dot(own[0:TOK], buf[...], ((1,), (0,)))
    out[...] = total + dot(oth[0:TOK], buf_o[...], ((1,), (0,)))


def first_kernel(q, got, near, *rest):
    out = rest[-1]
    half = TOK // 2
    ci = place()[1]
    hit = pl.ds(pl.multiple_of(ci * half, half), half)
    rest_rows = pl.ds(pl.multiple_of((1 - ci) * half, half), half)
    out[hit] = (near[hit] + got[0:half].astype(f32)).astype(bf16)
    out[rest_rows] = near[rest_rows].astype(bf16)
    if q == 0:
        own, oth = rest[:2]
        put_squares(out, TOK, unpack(own) + unpack(oth) + unpack(got, half))


def step_kernel(q, got, near, *rest):
    out = rest[-1]
    out[0:TOK] = (near[...] + got[0:TOK].astype(f32)).astype(bf16)
    if q == 0:
        own, oth = rest[:2]
        put_squares(out, TOK, unpack(own) + unpack(oth) + unpack(got))


def norm_kernel(own, oth, mine, out):
    out[...] = jnp.broadcast_to(unpack(own) + unpack(oth) + unpack(mine), (8, TOK))


def final_kernel(home, squares, *rest):
    out = rest[-1]
    n = SPLIT // 2
    swapped, kept = rest[:n], rest[n : 2 * n]
    total = squares[0:1] + unpack(swapped[0])
    scale = lax.rsqrt(total / (NZ * 2 * CH) + 1e-05)
    scale = jnp.broadcast_to(scale, (8, TOK)).T[:, 0:1]
    for q in range(n):
        tile = slice(q * WQ, (q + 1) * WQ)
        summed = home[:, tile] + kept[q][0:TOK].astype(f32) + swapped[q][0:TOK].astype(f32)
        out[:, tile] = (summed * scale).astype(bf16)


VM = pl.BlockSpec(memory_space=pltpu.VMEM)
SPACE = {"v": pltpu.VMEM, "p": pltpu.HBM, "h": pltpu.HBM}
SMALL = pltpu.CompilerParams(vmem_limit_bytes=12 * 2**20)
HB = pl.BlockSpec(memory_space=pltpu.HBM)


def near_by(value):
    return pltpu.with_memory_space_constraint(value, pltpu.VMEM)


def call(kernel, outs, ins, scratch=(), specs=None):
    specs = specs or "v" * len(ins)
    args, in_specs = [], []
    for kind, value in zip(specs, ins):
        args.append(pltpu.with_memory_space_constraint(value, SPACE[kind]))
        in_specs.append({"v": VM, "h": HB, "p": VM}[kind])
    return pl.pallas_call(
        kernel,
        out_shape=[pltpu.VMEM(shape, kind) for shape, kind in outs],
        in_specs=in_specs,
        out_specs=[VM] * len(outs),
        scratch_shapes=list(scratch),
        compiler_params=SMALL,
    )(*args)


def shards(x, z, bc, dt, decay_log, skip, conv_x, conv_bc, bias_x, bias_bc, gain, w):
    wide = CH + 2 * ST
    half = TOK // 2

    bo = other_core(bc)
    raw = [x, bc, dt.T, decay_log[None], conv_x, bias_x[None], conv_bc, bias_bc[None]]
    x, bc, *raw = call(
        load_kernel,
        [(v.shape, v.dtype) for v in raw],
        raw,
        [pltpu.SemaphoreType.DMA((len(raw),))],
        "h" * len(raw),
    )
    (tails,) = call(pack_tails_kernel, [((16, wide), bf16)], [x, bc, bo])
    tails = next_block(tails)
    xs, b, c, cum, dts, state, xh, bch, taps, bias = call(
        local_kernel,
        [
            ((TOK, CH), f32), ((TOK, ST), f32), ((TOK, ST), f32), ((TOK, HD), f32),
            ((TOK, HD), f32), ((CH, ST), f32), ((16, CH), f32), ((16, 2 * ST), f32),
            ((4, wide), f32), ((1, wide), f32),
        ],
        [x, bc, bo, *raw],
        [pltpu.VMEM((TOK + 16, CH), f32), pltpu.VMEM((TOK + 16, 2 * ST), f32)],
    )
    w_other = other_core(w)
    pay, first = call(
        tail_kernel,
        [((16, 48, ST), bf16), ((8, wide), f32)],
        [tails, xh, bch, cum, dts, state, taps, bias],
        [pltpu.VMEM((32, wide), f32)],
    )
    got = lax.all_to_all(pay, "ctx", 0, 0, tiled=True)
    a, e, ch, cl, gains = call(
        inner_kernel,
        [((TOK, CH), f32), ((TOK, CH), f32), ((TOK, ST), bf16), ((TOK, ST), bf16), ((1, CH), f32)],
        [xs, b, c, first, cum, dts, z, skip[None], gain[None]],
        (),
        "vvvvvvppp",
    )
    (back,) = call(scan_kernel, [((16, 32, ST), bf16)], [got])
    incoming = lax.all_to_all(back, "ctx", 0, 0, tiled=True)
    incoming = incoming.reshape(CH, ST)
    copies = [pltpu.SemaphoreType.DMA((2,))]
    far = call(fetch_kernel, [((CH, 2 * CH), bf16)] * 2, [w, w_other], copies, "hh")
    (hidden,) = call(gate_kernel, [((TOK + 16, CH), bf16)], [incoming, ch, cl, a, e, gains])
    pair = (hidden, other_core(hidden))

    def near(d):
        return call(
            partial(near_kernel, d),
            [((TOK, WQ), f32)] * SPLIT,
            [*pair, w, w_other],
            [pltpu.VMEM((CH, 2 * CH), bf16)] * 2 + copies,
            "vvhh",
        )

    def extra(rows, q):
        return ((rows + 16 if q == 0 else rows, WQ), bf16)

    def add(kernel, q, got, part):
        more = pair if q == 0 else ()
        return call(partial(kernel, q), [extra(TOK, q)], [got, part, *more])[0]

    sums = call(far_kernel, [extra(half, q) for q in range(SPLIT)], [*pair, *far])

    def hop():
        out = []
        for q in range(SPLIT):
            out.append(onward(sums[q]))
        return out

    for d in (3, 2, 1):
        sums = hop()
        part = near(d)
        kernel = first_kernel if d == 3 else step_kernel
        sums = [add(kernel, q, sums[q], part[q]) for q in range(SPLIT)]
    sums = hop()
    (home,) = call(
        home_kernel,
        [((TOK, CH), f32)],
        [*pair, w, w_other],
        [pltpu.VMEM((CH, CH), bf16)] * 2 + copies,
        "vvhh",
    )
    n = SPLIT // 2
    swapped = []
    for q in range(n):
        swapped.append(other_core(sums[q]))
    (squares,) = call(norm_kernel, [((8, TOK), f32)], [*pair, sums[0]])
    ins = [home, squares, *swapped, *sums[n:]]
    return pl.pallas_call(
        final_kernel,
        out_shape=jax.ShapeDtypeStruct((TOK, CH), bf16),
        in_specs=[VM] * len(ins),
        out_specs=VM,
        compiler_params=SMALL,
    )(*[near_by(v) for v in ins])


def solution(mesh):
    return jax.shard_map(
        shards,
        mesh=mesh,
        in_specs=(
            P("ctx", "tp"),
            P("ctx", "tp"),
            P("ctx", "tp"),
            P("ctx", "tp"),
            P("tp"),
            P("tp"),
            P(None, "tp"),
            P(),
            P("tp"),
            P(),
            P("tp"),
            P("tp", None),
        ),
        out_specs=P("ctx", "tp"),
        check_vma=False,
    )
```

```python
from functools import partial

import jax
import jax.numpy as jnp
from jax import lax
from jax.experimental import pallas as pl
from jax.experimental.pallas import tpu as pltpu
from jax.sharding import PartitionSpec as P


bf16 = jnp.bfloat16
f32 = jnp.float32
HIGH = lax.Precision.HIGHEST
AXES = ("ctx", "tp")
NX, NY, NZ = 4, 4, 8
TOK = 256
CH = 512
HD = 8
ST = 128
TILE = 128
SPLIT = 2
WQ = 2 * CH // SPLIT


def permute(value, target):
    pairs = []
    for ctx in range(NX * NY):
        for z in range(NZ):
            for c in range(2):
                to = target(ctx, z, c)
                if to is not None:
                    pairs.append((ctx * 16 + z * 2 + c, to[0] * 16 + (to[1] % NZ) * 2 + to[2]))
    return lax.ppermute(value, AXES, pairs)


def next_block(value):
    return permute(value, lambda k, z, c: (k + 1, z, c) if k < 15 else None)


def other_core(value):
    return permute(value, lambda k, z, c: (k, z, 1 - c))


def onward(value):
    return permute(value, lambda k, z, c: (k, z + 1 - 2 * c, c))


def place():
    rank = lax.axis_index("tp")
    return rank // 2, rank % 2


def silu(v):
    return v / (1.0 + jnp.exp(-v))


def dot(a, b, dims, precision=None):
    return lax.dot_general(a, b, (dims, ((), ())), precision=precision, preferred_element_type=f32)


def parts(v):
    high = v.astype(bf16)
    return high, (v - high.astype(f32)).astype(bf16)


def spread(cols, first):
    lane = lax.broadcasted_iota(jnp.int32, (cols.shape[0], TILE), 1)
    return jnp.where(lane < 64, cols[:, first : first + 1], cols[:, first + 1 : first + 2])


def conv(ref, tile, taps, bias, first, rows):
    total = bias
    for k in range(4):
        total = total + taps[k : k + 1] * ref[first - 3 + k : first - 3 + k + rows, tile]
    return silu(total)


def load_kernel(*refs):
    n = len(refs) // 2
    sem = refs[-1]
    copies = [pltpu.make_async_copy(refs[i], refs[n + i], sem.at[i]) for i in range(n)]
    for copy in copies:
        copy.start()
    for copy in copies:
        copy.wait()


def pack_tails_kernel(x, bc, bo, out):
    rows = slice(TOK - 16, TOK)
    out[:, 0:CH] = x[rows]
    out[:, CH : CH + ST] = bc[rows]
    out[:, CH + ST :] = bo[rows]


def carry_parts(last):
    carry = jnp.exp(last)
    value = jnp.concatenate([spread(carry, 2 * j) for j in range(4)], axis=1)
    high = value.astype(bf16).astype(f32)
    return high, value - high


def local_kernel(
    x, bc, bo, dt_t, dl, wx, bx, wbc, bbc,
    xs_out, b_out, c_out, cum_out, dts_out, pay, xh_out, bch_out, w_out, bias_out,
    joined, joined_bc,
):
    zi, ci = place()
    even = ci == 0
    joined[0:16] = jnp.zeros((16, CH), f32)
    joined[16:] = x[...].astype(f32)
    own, oth = bc[...].astype(f32), bo[...].astype(f32)
    joined_bc[0:16] = jnp.zeros((16, 2 * ST), f32)
    joined_bc[16:, 0:ST] = jnp.where(even, own, oth)
    joined_bc[16:, ST:] = jnp.where(even, oth, own)
    xh_out[...] = joined[16:32]
    bch_out[...] = joined_bc[16:32]
    group = pl.ds(pl.multiple_of(zi * 2 * ST, 2 * ST), 2 * ST)
    taps, bias = wbc[:, group], bbc[:, group]
    w_out[:, 0:CH] = wx[...]
    w_out[:, CH:] = taps
    bias_out[:, 0:CH] = bx[...]
    bias_out[:, CH:] = bias
    b = conv(joined_bc, slice(0, ST), taps[:, 0:ST], bias[:, 0:ST], 16, TOK)
    c = conv(joined_bc, slice(ST, 2 * ST), taps[:, ST:], bias[:, ST:], 16, TOK)
    b_out[...] = b
    c_out[...] = c
    dts = jnp.logaddexp(dt_t[...], 0.0).T
    dts_out[...] = dts
    row = lax.broadcasted_iota(jnp.int32, (TOK, TOK), 0)
    col = lax.broadcasted_iota(jnp.int32, (TOK, TOK), 1)
    cum = dot((row >= col).astype(f32), dts * -jnp.exp(dl[...]), ((1,), (0,)), HIGH)
    cum_out[...] = cum
    last = cum[TOK - 1 : TOK]
    closing = jnp.exp(last - cum) * dts
    late = lax.broadcasted_iota(jnp.int32, (TOK, HD), 0) >= 3
    closing = jnp.where(late, closing, 0.0)
    high, low = carry_parts(last)
    both = jnp.where(lax.broadcasted_iota(jnp.int32, (8, CH), 0) == 0, high, low)
    bh, bl = parts(b.T)
    over = ((1,), (0,))
    for j in range(2):
        weighted = []
        for i in (2 * j, 2 * j + 1):
            tile = slice(i * TILE, (i + 1) * TILE)
            xs = conv(joined, tile, wx[:, tile], bx[:, tile], 16, TOK)
            xs_out[:, tile] = xs
            weighted.append(xs * spread(closing, 2 * i))
        wh, wl = parts(jnp.concatenate(weighted, axis=1))
        cols = slice(2 * j * TILE, 2 * (j + 1) * TILE)
        state = dot(bh, wh, over) + (dot(bh, wl, over) + dot(bl, wh, over))
        for i in range(16):
            part = jnp.concatenate([state[8 * i : 8 * i + 8], both[:, cols]], axis=0)
            pay[i, :, cols] = part.astype(bf16)


def first_rows_kernel(tails, xh, bch, cum, dts, w, bias, first_out, info_out, joined):
    even = place()[1] == 0
    joined[0:16, 0:CH] = tails[:, 0:CH].astype(f32)
    own, oth = tails[:, CH : CH + ST].astype(f32), tails[:, CH + ST :].astype(f32)
    joined[0:16, CH : CH + ST] = jnp.where(even, own, oth)
    joined[0:16, CH + ST :] = jnp.where(even, oth, own)
    joined[16:32, 0:CH] = xh[...]
    joined[16:32, CH:] = bch[...]
    rows = conv(joined, slice(0, CH + 2 * ST), w[...], bias[...], 16, 8)
    first_out[...] = rows
    last = cum[TOK - 1 : TOK]
    closing = jnp.exp(last - cum[0:8]) * dts[0:8]
    b = rows[:, CH : CH + ST]
    spots = jnp.concatenate([b[0:1], b[1:2], b[2:3], jnp.zeros((1, ST), f32)], axis=1)
    v = jnp.concatenate([rows[:, j * TILE : (j + 1) * TILE] * spread(closing, 2 * j) for j in range(4)], axis=1)
    high, low = carry_parts(last)
    sub = lax.broadcasted_iota(jnp.int32, (8, CH), 0)
    rest = jnp.where(sub == 3, high, jnp.where(sub == 4, low, jnp.where(sub == 5, spots, 0.0)))
    info_out[...] = jnp.where(sub < 3, v, rest)


def patched(first, rest):
    return jnp.concatenate([first, rest[8:]], axis=0)


def inner_kernel(xs, b, c, first, cum, dts, z, sk, gain, a_out, e_out, ch_out, cl_out, gain_out):
    gain_out[...] = gain[...]
    cc = patched(first[:, CH + ST :], c[...])
    ch, cl = parts(cc)
    ch_out[...] = ch
    cl_out[...] = cl
    bh, bl = parts(patched(first[:, CH : CH + ST], b[...]))
    over = ((1,), (1,))
    cb = dot(ch, bh, over) + (dot(ch, bl, over) + dot(cl, bh, over))
    cum_c = cum[...]
    cum_r = cum_c.T
    grow = jnp.exp(cum_c)
    dts_c = dts[...]
    row = lax.broadcasted_iota(jnp.int32, (TILE, TILE), 0)
    lane = lax.broadcasted_iota(jnp.int32, (TILE, TILE), 1)
    lower = row >= lane
    half = (slice(0, TILE), slice(TILE, TOK))
    for j in range(4):
        tile = slice(j * TILE, (j + 1) * TILE)
        x_tile = patched(first[:, tile], xs[:, tile])
        x_dt = (x_tile * spread(dts_c, 2 * j)).astype(bf16)
        gate = silu(z[:, tile].astype(f32))
        grown = spread(grow, 2 * j)
        for i in range(2):
            ys = []
            for h in (2 * j, 2 * j + 1):
                cols = []
                for k in range(i + 1):
                    gap = cum_c[half[i], h : h + 1] - cum_r[h : h + 1, half[k]]
                    w = jnp.exp(jnp.minimum(gap, 0.0))
                    if k == i:
                        w = jnp.where(lower, w, 0.0)
                    cols.append((w * cb[half[i], half[k]]).astype(bf16))
                y = dot(cols[0], x_dt[half[0]], ((1,), (0,)))
                if i == 1:
                    y = y + dot(cols[1], x_dt[half[1]], ((1,), (0,)))
                ys.append(y)
            y = jnp.where(lane < 64, ys[0], ys[1])
            skip = jnp.where(lane[0:1] < 64, sk[:, 2 * j : 2 * j + 1], sk[:, 2 * j + 1 : 2 * j + 2])
            g = gate[half[i]]
            a_out[half[i], tile] = (y + skip * x_tile[half[i]]) * g
            e_out[half[i], tile] = grown[half[i]] * g


def scan_kernel(got, info, out):
    state = jnp.zeros((8, CH), f32)
    for k in range(16):
        out[k] = jnp.concatenate([state, info[...]], axis=0).astype(bf16)
        if k < 15:
            rows = got[k].astype(f32)
            state = (rows[8:9] + rows[9:10]) * state + rows[0:8]


def pack(total):
    high = total.astype(bf16).astype(f32)
    sub = lax.broadcasted_iota(jnp.int32, (16, TOK), 0)
    value = jnp.where(sub == 0, high, total - high)
    return jnp.where(sub < 2, value, 0.0).astype(bf16)


def unpack(ref, first=TOK):
    rows = ref[first : first + 16, 0:TOK].astype(f32)
    return rows[0:1] + rows[1:2]


def incoming_state(s):
    block = lax.axis_index("ctx")
    sub = lax.broadcasted_iota(jnp.int32, (8, CH), 0)
    near = sub[:, 0:ST]
    decay = jnp.ones((1, CH), f32)
    main, values, keys = [], [], []
    for i in reversed(range(16)):
        whole = s[i].astype(f32)
        rows = whole[8:16]
        main.append(whole[0:8])
        before = block > i
        values.append(jnp.where(sub < 3, rows, 0.0) * jnp.where(before, decay, 0.0))
        decay = jnp.where(before, decay * (rows[3:4] + rows[4:5]), decay)
        spots = rows[5:6]
        first = jnp.where(near == 0, spots[:, 0:ST], 0.0)
        second = jnp.where(near == 1, spots[:, ST : 2 * ST], 0.0)
        keys.append(first + second + jnp.where(near == 2, spots[:, 2 * ST : 3 * ST], 0.0))
    keys = jnp.concatenate(keys, axis=0).T.astype(bf16)
    extra = dot(keys, jnp.concatenate(values, axis=0).astype(bf16), ((1,), (0,)))
    return jnp.concatenate(main[::-1], axis=0).astype(bf16), extra.astype(bf16)


def gate_kernel(s, ch, cl, a, e, gain, h_out):
    main, extra = incoming_state(s)
    total = jnp.zeros((TOK, TILE), f32)
    over = ((1,), (0,))
    for j in range(4):
        tile = slice(j * TILE, (j + 1) * TILE)
        st = main[:, tile]
        carried = dot(ch[...], st, over) + (dot(cl[...], st, over) + dot(ch[...], extra[:, tile], over))
        gated = a[:, tile] + e[:, tile] * carried
        h_out[0:TOK, tile] = (gated * gain[:, tile]).astype(bf16)
        total = total + gated * gated
    h_out[TOK:, 0:TOK] = pack(jnp.sum(total.T, axis=0, keepdims=True))
    h_out[TOK:, TOK:] = jnp.zeros((16, CH - TOK), bf16)


def chip_block(d, w, buf, sem):
    zi, ci = place()
    at = (zi + d * (1 - 2 * ci)) & (NZ - 1)
    cols = pl.ds(pl.multiple_of(at * 2 * CH, 2 * CH), 2 * CH)
    return pltpu.make_async_copy(w.at[:, cols], buf, sem)


def fetch_kernel(w_own, w_oth, own_out, oth_out, sem):
    first = chip_block(4, w_own, own_out, sem.at[0])
    second = chip_block(4, w_oth, oth_out, sem.at[1])
    first.start()
    second.start()
    first.wait()
    second.wait()


def stream(q):
    side = (q * WQ) // CH
    ci = place()[1]
    return pl.ds(pl.multiple_of((ci ^ 1 ^ side) * CH + (q * WQ) % CH, WQ), WQ)


def half_rows():
    return pl.ds(pl.multiple_of(place()[1] * (TOK // 2), TOK // 2), TOK // 2)


def far_own_kernel(own, w_own, out):
    out[...] = dot(own[half_rows()], w_own[...], ((1,), (0,)))


def far_kernel(own, oth, begun, w_oth, *outs):
    lhs_o = oth[half_rows()]
    for q in range(SPLIT):
        at = stream(q)
        total = begun[:, at] + dot(lhs_o, w_oth[:, at], ((1,), (0,)))
        outs[q][0 : TOK // 2] = total.astype(bf16)
    squares = jnp.where(place()[1] == 0, unpack(own) + unpack(oth), 0.0)
    put_squares(outs[0], TOK // 2, squares)


def put_squares(out, first, squares):
    out[first:, 0:TOK] = pack(squares)
    if WQ > TOK:
        out[first:, TOK:] = jnp.zeros((16, WQ - TOK), bf16)


def near_kernel(d, own, oth, w_own, w_oth, *rest):
    outs, (buf, buf_o, sem) = rest[:SPLIT], rest[SPLIT:]
    first = chip_block(d, w_own, buf, sem.at[0])
    second = chip_block(d, w_oth, buf_o, sem.at[1])
    first.start()
    second.start()
    first.wait()
    second.wait()
    lhs, lhs_o = own[0:TOK], oth[0:TOK]
    for q in range(SPLIT):
        at = stream(q)
        outs[q][...] = dot(lhs, buf[:, at], ((1,), (0,))) + dot(lhs_o, buf_o[:, at], ((1,), (0,)))


def home_kernel(own, oth, w_own, w_oth, out, buf, buf_o, sem):
    zi, ci = place()
    cols = pl.ds(pl.multiple_of((zi * 2 + ci) * CH, CH), CH)
    first = pltpu.make_async_copy(w_own.at[:, cols], buf, sem.at[0])
    second = pltpu.make_async_copy(w_oth.at[:, cols], buf_o, sem.at[1])
    first.start()
    second.start()
    first.wait()
    second.wait()
    total = dot(own[0:TOK], buf[...], ((1,), (0,)))
    out[...] = total + dot(oth[0:TOK], buf_o[...], ((1,), (0,)))


def first_kernel(q, got, near, *rest):
    out = rest[-1]
    half = TOK // 2
    ci = place()[1]
    hit = pl.ds(pl.multiple_of(ci * half, half), half)
    rest_rows = pl.ds(pl.multiple_of((1 - ci) * half, half), half)
    out[hit] = (near[hit] + got[0:half].astype(f32)).astype(bf16)
    out[rest_rows] = near[rest_rows].astype(bf16)
    if q == 0:
        own, oth = rest[:2]
        put_squares(out, TOK, unpack(own) + unpack(oth) + unpack(got, half))


def step_kernel(q, got, near, *rest):
    out = rest[-1]
    out[0:TOK] = (near[...] + got[0:TOK].astype(f32)).astype(bf16)
    if q == 0:
        own, oth = rest[:2]
        put_squares(out, TOK, unpack(own) + unpack(oth) + unpack(got))


def norm_kernel(own, oth, mine, out):
    out[...] = jnp.broadcast_to(unpack(own) + unpack(oth) + unpack(mine), (8, TOK))


def final_kernel(home, squares, *rest):
    out = rest[-1]
    n = SPLIT // 2
    swapped, kept = rest[:n], rest[n : 2 * n]
    total = squares[0:1] + unpack(swapped[0])
    scale = lax.rsqrt(total / (NZ * 2 * CH) + 1e-05)
    scale = jnp.broadcast_to(scale, (8, TOK)).T[:, 0:1]
    for q in range(n):
        tile = slice(q * WQ, (q + 1) * WQ)
        summed = home[:, tile] + kept[q][0:TOK].astype(f32) + swapped[q][0:TOK].astype(f32)
        out[:, tile] = (summed * scale).astype(bf16)


VM = pl.BlockSpec(memory_space=pltpu.VMEM)
SPACE = {"v": pltpu.VMEM, "p": pltpu.HBM, "h": pltpu.HBM}
SMALL = pltpu.CompilerParams(vmem_limit_bytes=12 * 2**20)
HB = pl.BlockSpec(memory_space=pltpu.HBM)


def near_by(value):
    return pltpu.with_memory_space_constraint(value, pltpu.VMEM)


def call(kernel, outs, ins, scratch=(), specs=None):
    specs = specs or "v" * len(ins)
    args, in_specs = [], []
    for kind, value in zip(specs, ins):
        args.append(pltpu.with_memory_space_constraint(value, SPACE[kind]))
        in_specs.append({"v": VM, "h": HB, "p": VM}[kind])
    return pl.pallas_call(
        kernel,
        out_shape=[pltpu.VMEM(shape, kind) for shape, kind in outs],
        in_specs=in_specs,
        out_specs=[VM] * len(outs),
        scratch_shapes=list(scratch),
        compiler_params=SMALL,
    )(*args)


def shards(x, z, bc, dt, decay_log, skip, conv_x, conv_bc, bias_x, bias_bc, gain, w):
    wide = CH + 2 * ST
    half = TOK // 2

    bo = other_core(bc)
    raw = [x, bc, dt.T, decay_log[None], conv_x, bias_x[None], conv_bc, bias_bc[None]]
    x, bc, *raw = call(
        load_kernel,
        [(v.shape, v.dtype) for v in raw],
        raw,
        [pltpu.SemaphoreType.DMA((len(raw),))],
        "h" * len(raw),
    )
    xs, b, c, cum, dts, pay, xh, bch, taps, bias = call(
        local_kernel,
        [
            ((TOK, CH), f32), ((TOK, ST), f32), ((TOK, ST), f32), ((TOK, HD), f32),
            ((TOK, HD), f32), ((16, 16, CH), bf16), ((16, CH), f32), ((16, 2 * ST), f32),
            ((4, wide), f32), ((1, wide), f32),
        ],
        [x, bc, bo, *raw],
        [pltpu.VMEM((TOK + 16, CH), f32), pltpu.VMEM((TOK + 16, 2 * ST), f32)],
    )
    w_other = other_core(w)
    got = lax.all_to_all(pay, "ctx", 0, 0, tiled=True)
    (tails,) = call(pack_tails_kernel, [((16, wide), bf16)], [x, bc, bo])
    tails = next_block(tails)
    first, info = call(
        first_rows_kernel,
        [((8, wide), f32), ((8, CH), f32)],
        [tails, xh, bch, cum, dts, taps, bias],
        [pltpu.VMEM((32, wide), f32)],
    )
    a, e, ch, cl, gains = call(
        inner_kernel,
        [((TOK, CH), f32), ((TOK, CH), f32), ((TOK, ST), bf16), ((TOK, ST), bf16), ((1, CH), f32)],
        [xs, b, c, first, cum, dts, z, skip[None], gain[None]],
        (),
        "vvvvvvppp",
    )
    (back,) = call(scan_kernel, [((16, 16, CH), bf16)], [got, info])
    incoming = lax.all_to_all(back, "ctx", 0, 0, tiled=True)
    copies = [pltpu.SemaphoreType.DMA((2,))]
    far = call(fetch_kernel, [((CH, 2 * CH), bf16)] * 2, [w, w_other], copies, "hh")
    (hidden,) = call(gate_kernel, [((TOK + 16, CH), bf16)], [incoming, ch, cl, a, e, gains])
    pair = (hidden, other_core(hidden))

    def near(d):
        return call(
            partial(near_kernel, d),
            [((TOK, WQ), f32)] * SPLIT,
            [*pair, w, w_other],
            [pltpu.VMEM((CH, 2 * CH), bf16)] * 2 + copies,
            "vvhh",
        )

    def extra(rows, q):
        return ((rows + 16 if q == 0 else rows, WQ), bf16)

    def add(kernel, q, got, part):
        more = pair if q == 0 else ()
        return call(partial(kernel, q), [extra(TOK, q)], [got, part, *more])[0]

    (begun,) = call(far_own_kernel, [((half, 2 * CH), f32)], [hidden, far[0]])
    sums = call(far_kernel, [extra(half, q) for q in range(SPLIT)], [*pair, begun, far[1]])

    def hop():
        out = []
        for q in range(SPLIT):
            out.append(onward(sums[q]))
        return out

    for d in (3, 2, 1):
        sums = hop()
        part = near(d)
        kernel = first_kernel if d == 3 else step_kernel
        sums = [add(kernel, q, sums[q], part[q]) for q in range(SPLIT)]
    sums = hop()
    (home,) = call(
        home_kernel,
        [((TOK, CH), f32)],
        [*pair, w, w_other],
        [pltpu.VMEM((CH, CH), bf16)] * 2 + copies,
        "vvhh",
    )
    n = SPLIT // 2
    swapped = []
    for q in range(n):
        swapped.append(other_core(sums[q]))
    (squares,) = call(norm_kernel, [((8, TOK), f32)], [*pair, sums[0]])
    ins = [home, squares, *swapped, *sums[n:]]
    return pl.pallas_call(
        final_kernel,
        out_shape=jax.ShapeDtypeStruct((TOK, CH), bf16),
        in_specs=[VM] * len(ins),
        out_specs=VM,
        compiler_params=SMALL,
    )(*[near_by(v) for v in ins])


def solution(mesh):
    return jax.shard_map(
        shards,
        mesh=mesh,
        in_specs=(
            P("ctx", "tp"),
            P("ctx", "tp"),
            P("ctx", "tp"),
            P("ctx", "tp"),
            P("tp"),
            P("tp"),
            P(None, "tp"),
            P(),
            P("tp"),
            P(),
            P("tp"),
            P("tp", None),
        ),
        out_specs=P("ctx", "tp"),
        check_vma=False,
    )
```

```python
from functools import partial

import jax
import jax.numpy as jnp
from jax import lax
from jax.experimental import pallas as pl
from jax.experimental.pallas import tpu as pltpu
from jax.sharding import PartitionSpec as P


bf16 = jnp.bfloat16
f32 = jnp.float32
HIGH = lax.Precision.HIGHEST
AXES = ("ctx", "tp")
NX, NY, NZ = 4, 4, 8
TOK = 256
CH = 512
HD = 8
ST = 128
TILE = 128
SPLIT = 2
WQ = 2 * CH // SPLIT


def permute(value, target):
    pairs = []
    for ctx in range(NX * NY):
        for z in range(NZ):
            for c in range(2):
                to = target(ctx, z, c)
                if to is not None:
                    pairs.append((ctx * 16 + z * 2 + c, to[0] * 16 + (to[1] % NZ) * 2 + to[2]))
    return lax.ppermute(value, AXES, pairs)


def next_block(value):
    return permute(value, lambda k, z, c: (k + 1, z, c) if k < 15 else None)


def other_core(value):
    return permute(value, lambda k, z, c: (k, z, 1 - c))


def onward(value):
    return permute(value, lambda k, z, c: (k, z + 1 - 2 * c, c))


def place():
    rank = lax.axis_index("tp")
    return rank // 2, rank % 2


def silu(v):
    return v / (1.0 + jnp.exp(-v))


def dot(a, b, dims, precision=None):
    return lax.dot_general(a, b, (dims, ((), ())), precision=precision, preferred_element_type=f32)


def parts(v):
    high = v.astype(bf16)
    return high, (v - high.astype(f32)).astype(bf16)


def spread(cols, first):
    lane = lax.broadcasted_iota(jnp.int32, (cols.shape[0], TILE), 1)
    return jnp.where(lane < 64, cols[:, first : first + 1], cols[:, first + 1 : first + 2])


def conv(ref, tile, taps, bias, first, rows):
    total = bias
    for k in range(4):
        total = total + taps[k : k + 1] * ref[first - 3 + k : first - 3 + k + rows, tile]
    return silu(total)


def load_kernel(*refs):
    n = len(refs) // 2
    sem = refs[-1]
    copies = [pltpu.make_async_copy(refs[i], refs[n + i], sem.at[i]) for i in range(n)]
    for copy in copies:
        copy.start()
    for copy in copies:
        copy.wait()


def pack_tails_kernel(x, bc, bo, out):
    rows = slice(TOK - 16, TOK)
    out[:, 0:CH] = x[rows]
    out[:, CH : CH + ST] = bc[rows]
    out[:, CH + ST :] = bo[rows]


def carry_parts(last):
    carry = jnp.exp(last)
    value = jnp.concatenate([spread(carry, 2 * j) for j in range(4)], axis=1)
    high = value.astype(bf16).astype(f32)
    return high, value - high


def local_kernel(
    x, bc, bo, dt_t, dl, wx, bx, wbc, bbc,
    xs_out, b_out, c_out, cum_out, dts_out, pay, xh_out, bch_out, w_out, bias_out,
    joined, joined_bc,
):
    zi, ci = place()
    even = ci == 0
    joined[0:16] = jnp.zeros((16, CH), f32)
    joined[16:] = x[...].astype(f32)
    own, oth = bc[...].astype(f32), bo[...].astype(f32)
    joined_bc[0:16] = jnp.zeros((16, 2 * ST), f32)
    joined_bc[16:, 0:ST] = jnp.where(even, own, oth)
    joined_bc[16:, ST:] = jnp.where(even, oth, own)
    xh_out[...] = joined[16:32]
    bch_out[...] = joined_bc[16:32]
    group = pl.ds(pl.multiple_of(zi * 2 * ST, 2 * ST), 2 * ST)
    taps, bias = wbc[:, group], bbc[:, group]
    w_out[:, 0:CH] = wx[...]
    w_out[:, CH:] = taps
    bias_out[:, 0:CH] = bx[...]
    bias_out[:, CH:] = bias
    b = conv(joined_bc, slice(0, ST), taps[:, 0:ST], bias[:, 0:ST], 16, TOK)
    c = conv(joined_bc, slice(ST, 2 * ST), taps[:, ST:], bias[:, ST:], 16, TOK)
    b_out[...] = b
    c_out[...] = c
    dts = jnp.logaddexp(dt_t[...], 0.0).T
    dts_out[...] = dts
    row = lax.broadcasted_iota(jnp.int32, (TOK, TOK), 0)
    col = lax.broadcasted_iota(jnp.int32, (TOK, TOK), 1)
    cum = dot((row >= col).astype(f32), dts * -jnp.exp(dl[...]), ((1,), (0,)), HIGH)
    cum_out[...] = cum
    last = cum[TOK - 1 : TOK]
    closing = jnp.exp(last - cum) * dts
    late = lax.broadcasted_iota(jnp.int32, (TOK, HD), 0) >= 3
    closing = jnp.where(late, closing, 0.0)
    high, low = carry_parts(last)
    stack = [v[:, j * TILE : (j + 1) * TILE] for v in (high, low) for j in range(4)]
    both = jnp.concatenate(stack, axis=0).astype(bf16)
    for i in range(16):
        pay[i, :, CH:] = both
    bh, bl = parts(b.T)
    over = ((1,), (0,))
    for j in range(2):
        weighted = []
        for i in (2 * j, 2 * j + 1):
            tile = slice(i * TILE, (i + 1) * TILE)
            xs = conv(joined, tile, wx[:, tile], bx[:, tile], 16, TOK)
            xs_out[:, tile] = xs
            weighted.append(xs * spread(closing, 2 * i))
        wh, wl = parts(jnp.concatenate(weighted, axis=1))
        cols = slice(2 * j * TILE, 2 * (j + 1) * TILE)
        state = dot(bh, wh, over) + (dot(bh, wl, over) + dot(bl, wh, over))
        for i in range(16):
            pay[i, :, cols] = state[8 * i : 8 * i + 8].astype(bf16)


def first_rows_kernel(tails, xh, bch, cum, dts, w, bias, first_out, info_out, joined):
    even = place()[1] == 0
    joined[0:16, 0:CH] = tails[:, 0:CH].astype(f32)
    own, oth = tails[:, CH : CH + ST].astype(f32), tails[:, CH + ST :].astype(f32)
    joined[0:16, CH : CH + ST] = jnp.where(even, own, oth)
    joined[0:16, CH + ST :] = jnp.where(even, oth, own)
    joined[16:32, 0:CH] = xh[...]
    joined[16:32, CH:] = bch[...]
    rows = conv(joined, slice(0, CH + 2 * ST), w[...], bias[...], 16, 8)
    first_out[...] = rows
    last = cum[TOK - 1 : TOK]
    closing = jnp.exp(last - cum[0:8]) * dts[0:8]
    b = rows[:, CH : CH + ST]
    spots = jnp.concatenate([b[0:1], b[1:2], b[2:3], jnp.zeros((1, ST), f32)], axis=1)
    v = jnp.concatenate([rows[:, j * TILE : (j + 1) * TILE] * spread(closing, 2 * j) for j in range(4)], axis=1)
    high, low = carry_parts(last)
    sub = lax.broadcasted_iota(jnp.int32, (8, CH), 0)
    rest = jnp.where(sub == 3, high, jnp.where(sub == 4, low, jnp.where(sub == 5, spots, 0.0)))
    info_out[...] = jnp.where(sub < 3, v, rest)


def patched(first, rest):
    return jnp.concatenate([first, rest[8:]], axis=0)


def inner_kernel(xs, b, c, first, cum, dts, z, sk, gain, a_out, e_out, ch_out, cl_out, gain_out):
    gain_out[...] = gain[...]
    cc = patched(first[:, CH + ST :], c[...])
    ch, cl = parts(cc)
    ch_out[...] = ch
    cl_out[...] = cl
    bh, bl = parts(patched(first[:, CH : CH + ST], b[...]))
    over = ((1,), (1,))
    cb = dot(ch, bh, over) + (dot(ch, bl, over) + dot(cl, bh, over))
    cum_c = cum[...]
    cum_r = cum_c.T
    grow = jnp.exp(cum_c)
    dts_c = dts[...]
    row = lax.broadcasted_iota(jnp.int32, (TILE, TILE), 0)
    lane = lax.broadcasted_iota(jnp.int32, (TILE, TILE), 1)
    lower = row >= lane
    half = (slice(0, TILE), slice(TILE, TOK))
    for j in range(4):
        tile = slice(j * TILE, (j + 1) * TILE)
        x_tile = patched(first[:, tile], xs[:, tile])
        x_dt = (x_tile * spread(dts_c, 2 * j)).astype(bf16)
        gate = silu(z[:, tile].astype(f32))
        grown = spread(grow, 2 * j)
        for i in range(2):
            ys = []
            for h in (2 * j, 2 * j + 1):
                cols = []
                for k in range(i + 1):
                    gap = cum_c[half[i], h : h + 1] - cum_r[h : h + 1, half[k]]
                    w = jnp.exp(jnp.minimum(gap, 0.0))
                    if k == i:
                        w = jnp.where(lower, w, 0.0)
                    cols.append((w * cb[half[i], half[k]]).astype(bf16))
                y = dot(cols[0], x_dt[half[0]], ((1,), (0,)))
                if i == 1:
                    y = y + dot(cols[1], x_dt[half[1]], ((1,), (0,)))
                ys.append(y)
            y = jnp.where(lane < 64, ys[0], ys[1])
            skip = jnp.where(lane[0:1] < 64, sk[:, 2 * j : 2 * j + 1], sk[:, 2 * j + 1 : 2 * j + 2])
            g = gate[half[i]]
            a_out[half[i], tile] = (y + skip * x_tile[half[i]]) * g
            e_out[half[i], tile] = grown[half[i]] * g


def scan_kernel(got, info, out):
    state = jnp.zeros((8, CH), f32)
    for k in range(16):
        out[k] = jnp.concatenate([state, info[...]], axis=0).astype(bf16)
        if k < 15:
            rows = got[k].astype(f32)
            more = rows[:, CH:]
            carry = jnp.concatenate([more[j : j + 1] + more[j + 4 : j + 5] for j in range(4)], axis=1)
            state = carry * state + rows[:, 0:CH]


def pack(total):
    high = total.astype(bf16).astype(f32)
    sub = lax.broadcasted_iota(jnp.int32, (16, TOK), 0)
    value = jnp.where(sub == 0, high, total - high)
    return jnp.where(sub < 2, value, 0.0).astype(bf16)


def unpack(ref, first=TOK):
    rows = ref[first : first + 16, 0:TOK].astype(f32)
    return rows[0:1] + rows[1:2]


def incoming_state(s):
    block = lax.axis_index("ctx")
    sub = lax.broadcasted_iota(jnp.int32, (8, CH), 0)
    near = sub[:, 0:ST]
    decay = jnp.ones((1, CH), f32)
    main, values, keys = [], [], []
    for i in reversed(range(16)):
        whole = s[i].astype(f32)
        rows = whole[8:16]
        main.append(whole[0:8])
        before = block > i
        values.append(jnp.where(sub < 3, rows, 0.0) * jnp.where(before, decay, 0.0))
        decay = jnp.where(before, decay * (rows[3:4] + rows[4:5]), decay)
        spots = rows[5:6]
        first = jnp.where(near == 0, spots[:, 0:ST], 0.0)
        second = jnp.where(near == 1, spots[:, ST : 2 * ST], 0.0)
        keys.append(first + second + jnp.where(near == 2, spots[:, 2 * ST : 3 * ST], 0.0))
    keys = jnp.concatenate(keys, axis=0).T.astype(bf16)
    extra = dot(keys, jnp.concatenate(values, axis=0).astype(bf16), ((1,), (0,)))
    return jnp.concatenate(main[::-1], axis=0).astype(bf16), extra.astype(bf16)


def gate_kernel(s, ch, cl, a, e, gain, h_out):
    main, extra = incoming_state(s)
    total = jnp.zeros((TOK, TILE), f32)
    over = ((1,), (0,))
    for j in range(4):
        tile = slice(j * TILE, (j + 1) * TILE)
        st = main[:, tile]
        carried = dot(ch[...], st, over) + (dot(cl[...], st, over) + dot(ch[...], extra[:, tile], over))
        gated = a[:, tile] + e[:, tile] * carried
        h_out[0:TOK, tile] = (gated * gain[:, tile]).astype(bf16)
        total = total + gated * gated
    h_out[TOK:, 0:TOK] = pack(jnp.sum(total.T, axis=0, keepdims=True))
    h_out[TOK:, TOK:] = jnp.zeros((16, CH - TOK), bf16)


def chip_block(d, w, buf, sem):
    zi, ci = place()
    at = (zi + d * (1 - 2 * ci)) & (NZ - 1)
    cols = pl.ds(pl.multiple_of(at * 2 * CH, 2 * CH), 2 * CH)
    return pltpu.make_async_copy(w.at[:, cols], buf, sem)


def fetch_kernel(w_own, w_oth, own_out, oth_out, sem):
    first = chip_block(4, w_own, own_out, sem.at[0])
    second = chip_block(4, w_oth, oth_out, sem.at[1])
    first.start()
    second.start()
    first.wait()
    second.wait()


def stream(q):
    side = (q * WQ) // CH
    ci = place()[1]
    return pl.ds(pl.multiple_of((ci ^ 1 ^ side) * CH + (q * WQ) % CH, WQ), WQ)


def half_rows():
    return pl.ds(pl.multiple_of(place()[1] * (TOK // 2), TOK // 2), TOK // 2)


def far_own_kernel(own, w_own, out):
    out[...] = dot(own[half_rows()], w_own[...], ((1,), (0,)))


def far_kernel(own, oth, begun, w_oth, *outs):
    lhs_o = oth[half_rows()]
    for q in range(SPLIT):
        at = stream(q)
        total = begun[:, at] + dot(lhs_o, w_oth[:, at], ((1,), (0,)))
        outs[q][0 : TOK // 2] = total.astype(bf16)
    squares = jnp.where(place()[1] == 0, unpack(own) + unpack(oth), 0.0)
    put_squares(outs[0], TOK // 2, squares)


def put_squares(out, first, squares):
    out[first:, 0:TOK] = pack(squares)
    if WQ > TOK:
        out[first:, TOK:] = jnp.zeros((16, WQ - TOK), bf16)


def near_kernel(d, own, oth, w_own, w_oth, *rest):
    outs, (buf, buf_o, sem) = rest[:SPLIT], rest[SPLIT:]
    first = chip_block(d, w_own, buf, sem.at[0])
    second = chip_block(d, w_oth, buf_o, sem.at[1])
    first.start()
    second.start()
    first.wait()
    second.wait()
    lhs, lhs_o = own[0:TOK], oth[0:TOK]
    for q in range(SPLIT):
        at = stream(q)
        outs[q][...] = dot(lhs, buf[:, at], ((1,), (0,))) + dot(lhs_o, buf_o[:, at], ((1,), (0,)))


def home_kernel(own, oth, w_own, w_oth, out, buf, buf_o, sem):
    zi, ci = place()
    cols = pl.ds(pl.multiple_of((zi * 2 + ci) * CH, CH), CH)
    first = pltpu.make_async_copy(w_own.at[:, cols], buf, sem.at[0])
    second = pltpu.make_async_copy(w_oth.at[:, cols], buf_o, sem.at[1])
    first.start()
    second.start()
    first.wait()
    second.wait()
    total = dot(own[0:TOK], buf[...], ((1,), (0,)))
    out[...] = total + dot(oth[0:TOK], buf_o[...], ((1,), (0,)))


def first_kernel(q, got, near, *rest):
    out = rest[-1]
    half = TOK // 2
    ci = place()[1]
    hit = pl.ds(pl.multiple_of(ci * half, half), half)
    rest_rows = pl.ds(pl.multiple_of((1 - ci) * half, half), half)
    out[hit] = (near[hit] + got[0:half].astype(f32)).astype(bf16)
    out[rest_rows] = near[rest_rows].astype(bf16)
    if q == 0:
        own, oth = rest[:2]
        put_squares(out, TOK, unpack(own) + unpack(oth) + unpack(got, half))


def step_kernel(q, got, near, *rest):
    out = rest[-1]
    out[0:TOK] = (near[...] + got[0:TOK].astype(f32)).astype(bf16)
    if q == 0:
        own, oth = rest[:2]
        put_squares(out, TOK, unpack(own) + unpack(oth) + unpack(got))


def norm_kernel(own, oth, mine, out):
    out[...] = jnp.broadcast_to(unpack(own) + unpack(oth) + unpack(mine), (8, TOK))


def final_kernel(home, squares, *rest):
    out, buf, sem = rest[-3:]
    n = SPLIT // 2
    swapped, kept = rest[:n], rest[n : 2 * n]
    total = squares[0:1] + unpack(swapped[0])
    scale = lax.rsqrt(total / (NZ * 2 * CH) + 1e-05)
    scale = jnp.broadcast_to(scale, (8, TOK)).T[:, 0:1]
    copies = []
    for i in range(4):
        rows = slice(i * TOK // 4, (i + 1) * TOK // 4)
        for q in range(n):
            tile = slice(q * WQ, (q + 1) * WQ)
            summed = home[rows, tile] + kept[q][rows].astype(f32) + swapped[q][rows].astype(f32)
            buf[rows, tile] = (summed * scale[rows]).astype(bf16)
        copies.append(pltpu.make_async_copy(buf.at[rows], out.at[rows], sem.at[i]))
        copies[-1].start()
    for copy in copies:
        copy.wait()


VM = pl.BlockSpec(memory_space=pltpu.VMEM)
SPACE = {"v": pltpu.VMEM, "p": pltpu.HBM, "h": pltpu.HBM}
SMALL = pltpu.CompilerParams(vmem_limit_bytes=12 * 2**20)
HB = pl.BlockSpec(memory_space=pltpu.HBM)


def near_by(value):
    return pltpu.with_memory_space_constraint(value, pltpu.VMEM)


def call(kernel, outs, ins, scratch=(), specs=None):
    specs = specs or "v" * len(ins)
    args, in_specs = [], []
    for kind, value in zip(specs, ins):
        args.append(pltpu.with_memory_space_constraint(value, SPACE[kind]))
        in_specs.append({"v": VM, "h": HB, "p": VM}[kind])
    return pl.pallas_call(
        kernel,
        out_shape=[pltpu.VMEM(shape, kind) for shape, kind in outs],
        in_specs=in_specs,
        out_specs=[VM] * len(outs),
        scratch_shapes=list(scratch),
        compiler_params=SMALL,
    )(*args)


def shards(x, z, bc, dt, decay_log, skip, conv_x, conv_bc, bias_x, bias_bc, gain, w):
    wide = CH + 2 * ST
    half = TOK // 2

    bo = other_core(bc)
    raw = [x, bc, dt.T, decay_log[None], conv_x, bias_x[None], conv_bc, bias_bc[None]]
    x, bc, *raw = call(
        load_kernel,
        [(v.shape, v.dtype) for v in raw],
        raw,
        [pltpu.SemaphoreType.DMA((len(raw),))],
        "h" * len(raw),
    )
    xs, b, c, cum, dts, pay, xh, bch, taps, bias = call(
        local_kernel,
        [
            ((TOK, CH), f32), ((TOK, ST), f32), ((TOK, ST), f32), ((TOK, HD), f32),
            ((TOK, HD), f32), ((16, 8, CH + TILE), bf16), ((16, CH), f32), ((16, 2 * ST), f32),
            ((4, wide), f32), ((1, wide), f32),
        ],
        [x, bc, bo, *raw],
        [pltpu.VMEM((TOK + 16, CH), f32), pltpu.VMEM((TOK + 16, 2 * ST), f32)],
    )
    w_other = other_core(w)
    got = lax.all_to_all(pay, "ctx", 0, 0, tiled=True)
    (tails,) = call(pack_tails_kernel, [((16, wide), bf16)], [x, bc, bo])
    tails = next_block(tails)
    first, info = call(
        first_rows_kernel,
        [((8, wide), f32), ((8, CH), f32)],
        [tails, xh, bch, cum, dts, taps, bias],
        [pltpu.VMEM((32, wide), f32)],
    )
    a, e, ch, cl, gains = call(
        inner_kernel,
        [((TOK, CH), f32), ((TOK, CH), f32), ((TOK, ST), bf16), ((TOK, ST), bf16), ((1, CH), f32)],
        [xs, b, c, first, cum, dts, z, skip[None], gain[None]],
        (),
        "vvvvvvppp",
    )
    (back,) = call(scan_kernel, [((16, 16, CH), bf16)], [got, info])
    incoming = lax.all_to_all(back, "ctx", 0, 0, tiled=True)
    copies = [pltpu.SemaphoreType.DMA((2,))]
    far = call(fetch_kernel, [((CH, 2 * CH), bf16)] * 2, [w, w_other], copies, "hh")
    (hidden,) = call(gate_kernel, [((TOK + 16, CH), bf16)], [incoming, ch, cl, a, e, gains])
    pair = (hidden, other_core(hidden))

    def near(d):
        return call(
            partial(near_kernel, d),
            [((TOK, WQ), f32)] * SPLIT,
            [*pair, w, w_other],
            [pltpu.VMEM((CH, 2 * CH), bf16)] * 2 + copies,
            "vvhh",
        )

    def extra(rows, q):
        return ((rows + 16 if q == 0 else rows, WQ), bf16)

    def add(kernel, q, got, part):
        more = pair if q == 0 else ()
        return call(partial(kernel, q), [extra(TOK, q)], [got, part, *more])[0]

    (begun,) = call(far_own_kernel, [((half, 2 * CH), f32)], [hidden, far[0]])
    sums = call(far_kernel, [extra(half, q) for q in range(SPLIT)], [*pair, begun, far[1]])

    def hop():
        out = []
        for q in range(SPLIT):
            out.append(onward(sums[q]))
        return out

    for d in (3, 2, 1):
        sums = hop()
        part = near(d)
        kernel = first_kernel if d == 3 else step_kernel
        sums = [add(kernel, q, sums[q], part[q]) for q in range(SPLIT)]
    sums = hop()
    (home,) = call(
        home_kernel,
        [((TOK, CH), f32)],
        [*pair, w, w_other],
        [pltpu.VMEM((CH, CH), bf16)] * 2 + copies,
        "vvhh",
    )
    n = SPLIT // 2
    swapped = []
    for q in range(n):
        swapped.append(other_core(sums[q]))
    (squares,) = call(norm_kernel, [((8, TOK), f32)], [*pair, sums[0]])
    ins = [home, squares, *swapped, *sums[n:]]
    return pl.pallas_call(
        final_kernel,
        out_shape=jax.ShapeDtypeStruct((TOK, CH), bf16),
        in_specs=[VM] * len(ins),
        out_specs=HB,
        scratch_shapes=[pltpu.VMEM((TOK, CH), bf16), pltpu.SemaphoreType.DMA((4,))],
        compiler_params=SMALL,
    )(*[near_by(v) for v in ins])


def solution(mesh):
    return jax.shard_map(
        shards,
        mesh=mesh,
        in_specs=(
            P("ctx", "tp"),
            P("ctx", "tp"),
            P("ctx", "tp"),
            P("ctx", "tp"),
            P("tp"),
            P("tp"),
            P(None, "tp"),
            P(),
            P("tp"),
            P(),
            P("tp"),
            P("tp", None),
        ),
        out_specs=P("ctx", "tp"),
        check_vma=False,
    )
```
